32 devices in a mesh: lat: 4 (over y, x), lon: 8 (over z, core).
Axes of the slice: x: 2, y: 2, z: 4, core: 2. Of those that a mesh axis runs over, the one named last changes fastest.
Arguments:
- grad_rows: bfloat16 [32768, 128], P(('lat', 'lon')), may hold values from -6 to 6
- owner: int32 [32768, 1], P(('lat', 'lon')), may hold values from 0 to 31; in each aligned block of 1024 rows (0 to 1023, 1024 to 2047, ...) at most 64 rows name the same one
- lat_offset: int32 [32768], P(('lat', 'lon')), may hold values from 0 to 63
- lon_offset: int32 [32768], P(('lat', 'lon')), may hold values from 0 to 127
- position: bfloat16 [32768, 2], P(('lat', 'lon')), may hold values from 0 to 1
- live_count: int32 [32], P(('lat', 'lon')), may hold values from 512 to 1024
- features: bfloat16 [256, 1024, 128], P('lat', 'lon'), may hold values from -6 to 6
- conv_weight: bfloat16 [3, 3, 128, 128], replicated, may hold values from -0.1875 to 0.1875
Outputs:
- input_grad: bfloat16 [256, 1024, 128], P('lat', 'lon')
- weight_grad: float32 [3, 3, 128, 128], replicated
The draws below stay inside these ranges and needn't reach their ends.
Inputs may be any that keep to these rules, and one draw needn't show every extreme that they name: `owner`: among the 1024 rows of one device no tile is named more than 64 times, a bound that some block reaches. `live_count`: entry k counts the real rows among the rows of device k, which come first.
All inputs are finite; a program needn't handle non-finite values.
Results may differ from the reference program's by a relative error of at most 0.012.
Values may be sent and summed in bfloat16 or wider, within the bound.
A program may use at most 128 MiB of HBM per device.

```python
import math
import jax
import jax.numpy as jnp
import numpy as np
from jax import lax

C = 128
CLAT = 64
CLON = 128
ROWS_DEV = 1024
CAP = 64
NLAT = 256
NLON = 1024
ROWS = 32768
N_LAT = 4
N_LON = 8


def with_ends(drawn, key, least, largest):
    longest = drawn.shape.index(max(drawn.shape))
    spots = []
    for shift in (0, 1):
        where = [jax.random.randint(jax.random.fold_in(key, axis), (), 0, length) for axis, length in enumerate(drawn.shape)]
        where[longest] = (where[longest] + shift) % drawn.shape[longest]
        spots.append(tuple(where))
    return drawn.at[spots[0]].set(least).at[spots[1]].set(largest)


def block_levels(own_key, shape, pieces, smallest, high):
    def one(dim, blocks):
        steps = jax.random.uniform(jax.random.fold_in(jax.random.fold_in(own_key, 6), dim), (blocks,), jnp.float32, smallest / len(pieces), high / len(pieces))
        return jnp.repeat(jnp.exp(steps), shape[dim] // blocks).reshape((-1,) + (1,) * (len(shape) - dim - 1))

    loudness = one(*pieces[0])
    for cut in pieces[1:]:
        loudness = loudness * one(*cut)
    return loudness


def deal_out(own_key, own, number, rows, number_of, top, limit, skew):
    order = jax.random.permutation(own_key, number_of)
    packed, usual = portions_of(number_of, rows * top, limit, skew, True), portions_of(number_of, rows * top, limit, skew, False)
    places = jnp.arange(number_of)

    def named(tallies, offset_by):
        used = int((tallies > 0).sum())
        fixed = max(1, used // 4)
        moved = fixed + (places - fixed + offset_by * (used - fixed)) % max(1, number_of - fixed)
        return jnp.zeros((number_of,), jnp.int32).at[order[jnp.where(places < fixed, places, moved)]].set(jnp.asarray(tallies, jnp.int32))

    tallies = jnp.where(number % 4 == 0, named(packed, number // 4), named(usual, number - number // 4 - 1))
    mixed = jax.random.permutation(jax.random.fold_in(own, 3), number_of)
    giver, receiver = mixed[0:number_of // 2 * 2:2], mixed[1:number_of // 2 * 2:2]
    room = jnp.minimum(tallies[giver] - 1, limit - tallies[receiver]) // 2
    room = jnp.where((giver == order[0]) | (receiver == order[0]) | (tallies[receiver] == 0), 0, jnp.maximum(room, 0))
    moved = jax.random.randint(jax.random.fold_in(own, 4), (number_of // 2,), 0, 1 << 20) % (room + 1)
    tallies = tallies.at[giver].add(-moved).at[receiver].add(moved)
    labels = jnp.searchsorted(jnp.cumsum(tallies), jnp.arange(rows * top), side="right").astype(jnp.int32)
    grid = labels.reshape(top, rows).T
    grid = grid[jax.random.permutation(jax.random.fold_in(own, 1), rows)]
    offset_by = jax.random.randint(jax.random.fold_in(own, 2), (rows, 1), 0, top)
    return jnp.take_along_axis(grid, (jnp.arange(top)[None, :] + offset_by) % top, axis=1)


def portions_of(number_of, total, reach, skew, full):
    portions = [(1 << 20) // math.isqrt(grade ** skew) + 1 for grade in range(1, number_of + 1)]
    largest = reach if full else min(reach, max(-(-total // number_of), total * portions[0] // sum(portions)))
    least = 1 if total - largest >= number_of - 1 else 0
    counts, rest = [largest] + [least] * (number_of - 1), total - largest - least * (number_of - 1)
    while rest > 0:
        movable = [i for i in range(1, number_of) if counts[i] < largest] or [i for i in range(1, number_of) if counts[i] < reach]
        whole, remaining = sum([portions[i] for i in movable]), rest
        for i in movable:
            more = min(reach - counts[i], max(1, remaining * portions[i] // whole), rest)
            counts[i] = counts[i] + more
            rest = rest - more
    return np.array(counts)


def noise(rng, extent, scale, reach, shards=(), kind=jnp.bfloat16):
    drawn = scale * jax.random.normal(rng, extent, jnp.float32)
    if shards:
        drawn = drawn * block_levels(rng, extent, shards, -0.22, 0.18)
    return jnp.clip(drawn, -reach, reach).astype(kind)


def setup_inputs(seed: int = 0) -> dict:
    key_list = jax.random.split(jax.random.key(seed), 9)
    grad_rows = noise(key_list[0], (ROWS, C), 1.0, 6.0, ((0, 32),))
    owner_keys = jax.random.split(jax.random.fold_in(key_list[1], 1), ROWS // ROWS_DEV)
    owner_turns = jax.random.permutation(jax.random.fold_in(key_list[1], 3), ROWS // ROWS_DEV)
    owner = jax.vmap(lambda own, number: deal_out(jax.random.fold_in(key_list[1], 2), own, number, ROWS_DEV, N_LAT * N_LON, 1, CAP, 2))(owner_keys, owner_turns).reshape((ROWS, 1))
    lat_offset = with_ends(jax.random.randint(key_list[2], (ROWS,), 0, CLAT), jax.random.fold_in(key_list[2], 1), 0, CLAT - 1).astype(jnp.int32)
    lon_offset = with_ends(jax.random.randint(key_list[3], (ROWS,), 0, CLON), jax.random.fold_in(key_list[3], 1), 0, CLON - 1).astype(jnp.int32)
    position = jnp.clip(1.0 * jax.random.uniform(key_list[4], (ROWS, 2), jnp.float32) ** block_levels(key_list[4], (ROWS, 2), ((0, 32),), -0.2, 0.2), 0.0, 1.0).astype(jnp.bfloat16)
    live_count = with_ends(jax.random.randint(key_list[5], (N_LAT * N_LON,), ROWS_DEV // 2, ROWS_DEV + 1), jax.random.fold_in(key_list[5], 1), ROWS_DEV // 2, ROWS_DEV).astype(jnp.int32)
    features = noise(key_list[6], (NLAT, NLON, C), 1.0, 6.0, ((0, 4), (1, 8)))
    conv_weight = noise(key_list[7], (3, 3, C, C), (9 * C) ** -0.5, 0.1875)
    return {"grad_rows": grad_rows, "owner": owner, "lat_offset": lat_offset, "lon_offset": lon_offset, "position": position, "live_count": live_count, "features": features, "conv_weight": conv_weight}


rbf_scale = 1.5


def profile(frac):
    tap_index = jnp.arange(8).astype(frac.dtype)
    return jnp.exp(-jnp.square(tap_index[None, :] - 3.0 - frac[:, None]) / (2.0 * rbf_scale * rbf_scale))


def reference(grad_rows, owner, lat_offset, lon_offset, position, live_count, features, conv_weight):
    row_total = grad_rows.shape[0]
    row_ids = jnp.arange(row_total, dtype=jnp.int32)
    is_live = (row_ids % ROWS_DEV) < live_count[row_ids // ROWS_DEV]
    owner_tile = owner[:, 0]
    base_lat = (owner_tile // N_LON) * CLAT + lat_offset - 3
    base_lon = (owner_tile % N_LON) * CLON + lon_offset - 3
    tap_ints = jnp.arange(8, dtype=jnp.int32)
    lat_cell = base_lat[:, None] + tap_ints[None, :]
    lon_cell = (base_lon[:, None] + tap_ints[None, :]) % NLON
    valid = (lat_cell >= 0) & (lat_cell < NLAT) & is_live[:, None]
    cell_index = jnp.where(valid[:, :, None], lat_cell[:, :, None] * NLON + lon_cell[:, None, :], NLAT * NLON).astype(jnp.int32)
    lat_weight = profile(position[:, 0].astype(jnp.float32)).astype(jnp.bfloat16)
    lon_weight = profile(position[:, 1].astype(jnp.float32)).astype(jnp.bfloat16)
    block_rows = math.gcd(row_total, 8192)
    blocks = row_total // block_rows

    def accumulate(canvas, payload):
        rows_blk, lat_blk, lon_blk, index_blk = payload
        spread = lon_blk[:, :, None] * rows_blk[:, None, :]
        updates = lat_blk.astype(jnp.float32)[:, :, None, None] * spread.astype(jnp.float32)[:, None, :, :]
        canvas = canvas.at[index_blk.reshape(-1)].add(updates.reshape(-1, C), mode="drop")
        return canvas, None

    canvas, _ = lax.scan(accumulate, jnp.zeros((NLAT * NLON, C), jnp.float32),
                         (grad_rows.reshape(blocks, block_rows, C), lat_weight.reshape(blocks, block_rows, 8),
                          lon_weight.reshape(blocks, block_rows, 8), cell_index.reshape(blocks, block_rows, 8, 8)))
    grid_grad = canvas.reshape(NLAT, NLON, C).astype(jnp.bfloat16)

    def pad_grid(field):
        padded = jnp.pad(field, ((1, 1), (0, 0), (0, 0)))
        return jnp.concatenate([padded[:, -1:], padded, padded[:, :1]], axis=1)

    grid_padded = pad_grid(grid_grad)
    input_padded = pad_grid(features)
    flat_grad = grid_grad.reshape(-1, C)
    input_grad = jnp.zeros((NLAT * NLON, C), jnp.float32)
    weight_parts = []
    for a in range(3):
        for b in range(3):
            shifted = grid_padded[2 - a:2 - a + NLAT, 2 - b:2 - b + NLON].reshape(-1, C)
            input_grad = input_grad + jnp.dot(shifted, conv_weight[a, b].T, preferred_element_type=jnp.float32)
            window = input_padded[a:a + NLAT, b:b + NLON].reshape(-1, C)
            weight_parts.append(jnp.dot(window.T, flat_grad, preferred_element_type=jnp.float32))
    weight_grad = jnp.stack(weight_parts).reshape(3, 3, C, C)
    return input_grad.reshape(NLAT, NLON, C).astype(jnp.bfloat16), weight_grad
```

```python
import functools
import math

import jax
import jax.numpy as jnp
from jax import lax
from jax.experimental import pallas as pl
from jax.experimental.pallas import tpu as pltpu
from jax.sharding import PartitionSpec as P

rbf_scale = 1.5
taps = 8
before = 3
after = taps - 1 - before
geom_rows = 8
f32 = jnp.float32
bf16 = jnp.bfloat16


def pack_kernel(capacity, live_ref, rows_ref, owner_ref, lat_ref, lon_ref, pos_ref, out_ref):
    devices = out_ref.shape[0]
    row_total = rows_ref.shape[0]
    live = lax.broadcasted_iota(jnp.int32, (1, row_total), 1) < live_ref[0]
    owner = jnp.where(live, owner_ref[...], devices)
    match = lax.broadcasted_iota(jnp.int32, (devices, row_total), 0) == owner
    match = jnp.where(match, 1.0, 0.0)
    upper = lax.broadcasted_iota(jnp.int32, (row_total, row_total), 0) < lax.broadcasted_iota(
        jnp.int32, (row_total, row_total), 1
    )
    upper = jnp.where(upper, 1.0, 0.0).astype(bf16)
    earlier = jnp.dot(match.astype(bf16), upper, preferred_element_type=f32)
    rank = jnp.sum(earlier * match, axis=0, keepdims=True).astype(jnp.int32)
    slot = owner * capacity + rank
    geometry = jnp.concatenate(
        [
            pos_ref[...].astype(f32),
            lat_ref[...].astype(f32),
            lon_ref[...].astype(f32),
            jnp.where(live, 1.0, 0.0),
            jnp.zeros((geom_rows - 5, row_total), f32),
        ],
        axis=0,
    ).astype(bf16)
    group = max(1, min(devices, 256 // capacity))
    line = lax.broadcasted_iota(jnp.int32, (group * capacity, row_total), 0)
    for first in range(0, devices, group):
        hit = jnp.where(line == slot - first * capacity, 1.0, 0.0).astype(bf16)
        placed = jnp.dot(hit, rows_ref[...], preferred_element_type=f32).astype(bf16)
        info = lax.dot_general(
            geometry, hit, (((1,), (1,)), ((), ())), preferred_element_type=f32
        ).astype(bf16)
        for i in range(group):
            out_ref[first + i, 0:capacity, :] = placed[i * capacity : (i + 1) * capacity]
            out_ref[first + i, capacity : capacity + geom_rows, 0:capacity] = info[
                :, i * capacity : (i + 1) * capacity
            ]


def scatter_kernel(
    capacity,
    lanes,
    count_ref,
    lat_ref,
    lon_ref,
    fa_ref,
    fb_ref,
    msg_ref,
    own_ref,
    up_ref,
    down_ref,
    left_ref,
    right_ref,
    canvas,
    block,
):
    sources = msg_ref.shape[0]
    rows, cols = own_ref.shape[0], own_ref.shape[1]
    tall = canvas.shape[1]
    inv = 1.0 / (2.0 * rbf_scale * rbf_scale)

    def clear(i, _):
        for j in range(lanes):
            canvas[j, i] = jnp.zeros(canvas.shape[2:], f32)
        return 0

    lax.fori_loop(0, tall, clear, 0)
    line = lax.broadcasted_iota(jnp.int32, (taps, canvas.shape[3]), 0).astype(f32) - before
    level = [math.exp(-((a - before) ** 2 - before**2) * inv) for a in range(taps)]

    def source(src, _):
        block[...] = msg_ref[src, 0:capacity, :].astype(f32)

        def step(i, _):
            terms = []
            for j in range(lanes):
                s = i * lanes + j
                at = src * capacity + s
                fa = fa_ref[at]
                d = line - fb_ref[at]
                t = jnp.exp(-(d * d + (before + fa) * (before + fa)) * inv) * block[pl.ds(s, 1), :]
                g = jnp.exp(jnp.full(t.shape, 2.0 * inv, f32) * fa)
                terms.append((lat_ref[at], lon_ref[at], t, g))
            sums = []
            for j, (r, c, t, g) in enumerate(terms):
                for a in range(taps):
                    sums.append(canvas[j, r + a, pl.ds(c, taps), :] + t * level[a])
                    t = t * g
            for j, (r, c, _, _) in enumerate(terms):
                for a in range(taps):
                    canvas[j, r + a, pl.ds(c, taps), :] = sums[j * taps + a]
            return 0

        lax.fori_loop(0, (count_ref[src] + lanes - 1) // lanes, step, 0)
        return 0

    lax.fori_loop(0, sources, source, 0)
    up, down = before + 1, after + 1
    inset = before - 1

    def total(i):
        whole = canvas[0, i]
        for j in range(1, lanes):
            whole = whole + canvas[j, i]
        canvas[0, i] = whole

    def finish(i, _):
        total(i)
        return 0

    lax.fori_loop(0, tall, finish, 0)

    def emit(i, _):
        own_ref[i] = canvas[0, i + inset, inset : inset + cols, :].astype(bf16)
        left_ref[i] = canvas[0, i + inset, 0:up, :].astype(bf16)
        right_ref[i] = canvas[0, i + inset, inset + cols - 2 : inset + cols - 2 + down, :].astype(bf16)
        return 0

    lax.fori_loop(0, rows, emit, 0)
    for i in range(up):
        up_ref[i] = canvas[0, i].astype(bf16)
    for i in range(down):
        down_ref[i] = canvas[0, inset + rows - 2 + i].astype(bf16)


def conv_kernel(
    edge_ref,
    own_ref,
    up_ref,
    down_ref,
    left_ref,
    right_ref,
    ul_ref,
    ur_ref,
    dl_ref,
    dr_ref,
    feat_ref,
    weight_ref,
    ig_ref,
    wg_ref,
    grid,
    windows,
    turned,
    total,
):
    rows, cols = own_ref.shape[0], own_ref.shape[1]
    tile_lat, tile_lon, channels = feat_ref.shape
    up, down = before + 1, after + 1
    inset = before - 1

    def fill(i, _):
        grid[i, 0:cols, :] = own_ref[i].astype(f32)
        grid[i, 0:down, :] += right_ref[i].astype(f32)
        grid[i, cols - up : cols, :] += left_ref[i].astype(f32)
        return 0

    lax.fori_loop(0, rows, fill, 0)
    for i in range(up):
        at = rows - up + i
        grid[at, 0:cols, :] += up_ref[i, inset : inset + cols, :].astype(f32)
        grid[at, cols - up : cols, :] += ul_ref[i].astype(f32)
        grid[at, 0:down, :] += ur_ref[i].astype(f32)
    for i in range(down):
        grid[i, 0:cols, :] += down_ref[i, inset : inset + cols, :].astype(f32)
        grid[i, cols - up : cols, :] += dl_ref[i].astype(f32)
        grid[i, 0:down, :] += dr_ref[i].astype(f32)

    @pl.when(edge_ref[0] == 0)
    def _():
        grid[0] = jnp.zeros(grid.shape[1:], f32)

    @pl.when(edge_ref[0] == edge_ref[1] - 1)
    def _():
        grid[rows - 1] = jnp.zeros(grid.shape[1:], f32)

    def shift(i, _):
        for b in range(3):
            windows[pl.ds(pl.multiple_of(i * tile_lon, tile_lon), tile_lon), b * channels : (b + 1) * channels] = grid[
                i, 2 - b : 2 - b + tile_lon, :
            ].astype(bf16)
        return 0

    lax.fori_loop(0, rows, shift, 0)
    turned[:, 0 : 2 * tile_lon] = jnp.zeros((channels, 2 * tile_lon), bf16)
    turned[:, rows * tile_lon : (rows + 2) * tile_lon] = jnp.zeros((channels, 2 * tile_lon), bf16)

    def turn(p, _):
        turned[:, pl.ds(pl.multiple_of((p + 2) * tile_lon, tile_lon), tile_lon)] = feat_ref[p].T
        return 0

    lax.fori_loop(0, tile_lat, turn, 0)
    step = next(n for n in (11, 6, 3, 2, 1) if rows % n == 0)
    depth = step * tile_lon
    total[...] = jnp.zeros_like(total)

    def weigh(k, _):
        start = k * depth
        lhs = jnp.concatenate(
            [
                turned[:, pl.ds(pl.multiple_of(start + a * tile_lon, tile_lon), depth)]
                for a in range(3)
            ],
            axis=0,
        )
        rhs = windows[pl.ds(pl.multiple_of(start, tile_lon), depth), :]
        total[...] += jnp.dot(lhs, rhs, preferred_element_type=f32)
        return 0

    lax.fori_loop(0, rows // step, weigh, 0)
    for a in range(3):
        for b in range(3):
            wg_ref[a, b] = total[
                a * channels : (a + 1) * channels, b * channels : (b + 1) * channels
            ].astype(wg_ref.dtype)
    part = math.gcd(tile_lat, 8)

    def apply(k, _):
        acc = jnp.zeros((part * tile_lon, channels), f32)
        for a in range(3):
            start = pl.multiple_of((k * part + 2 - a) * tile_lon, tile_lon)
            acc = acc + jnp.dot(
                windows[pl.ds(start, part * tile_lon), :], weight_ref[a], preferred_element_type=f32
            )
        ig_ref[pl.ds(k * part, part)] = acc.reshape(part, tile_lon, channels).astype(bf16)
        return 0

    lax.fori_loop(0, tile_lat // part, apply, 0)


def shards(grad_rows, owner, lat_offset, lon_offset, position, live_count, features, conv_weight):
    lat_total = lax.axis_size("lat")
    lon_total = lax.axis_size("lon")
    device_total = lat_total * lon_total
    row_total, channels = grad_rows.shape
    tile_lat, tile_lon = features.shape[:2]
    capacity = max(2, 2 * row_total // device_total)
    smem = pl.BlockSpec(memory_space=pltpu.SMEM)
    vmem = pl.BlockSpec(memory_space=pltpu.VMEM)
    axes = ("lat", "lon")

    outgoing = pl.pallas_call(
        functools.partial(pack_kernel, capacity),
        out_shape=jax.ShapeDtypeStruct((device_total, capacity + geom_rows, channels), bf16),
        in_specs=[smem] + [vmem] * 5,
        out_specs=vmem,
        name="pack",
    )(
        live_count,
        grad_rows,
        owner.reshape(1, row_total),
        lat_offset.reshape(1, row_total),
        lon_offset.reshape(1, row_total),
        position.T,
    )
    incoming = lax.all_to_all(outgoing, axes, split_axis=0, concat_axis=0, tiled=True)
    info = incoming[:, capacity : capacity + 5, :capacity].astype(f32).transpose(1, 0, 2)
    counts = jnp.sum(info[4], axis=1).astype(jnp.int32)
    info = info.reshape(5, -1)

    rows, cols = tile_lat + 2, tile_lon + 2
    tall = tile_lat + taps - 1
    wide = -(-(tile_lon + taps - 1) // 8) * 8
    up, down = before + 1, after + 1
    lanes = math.gcd(capacity, 4)
    own, up_s, down_s, left_s, right_s = pl.pallas_call(
        functools.partial(scatter_kernel, capacity, lanes),
        out_shape=[
            jax.ShapeDtypeStruct((rows, cols, channels), bf16),
            jax.ShapeDtypeStruct((up, wide, channels), bf16),
            jax.ShapeDtypeStruct((down, wide, channels), bf16),
            jax.ShapeDtypeStruct((rows, up, channels), bf16),
            jax.ShapeDtypeStruct((rows, down, channels), bf16),
        ],
        in_specs=[smem] * 5 + [vmem],
        out_specs=[vmem] * 5,
        scratch_shapes=[
            pltpu.VMEM((lanes, tall, wide, channels), f32),
            pltpu.VMEM((capacity, channels), f32),
        ],
        compiler_params=pltpu.CompilerParams(vmem_limit_bytes=60 * 2**20),
        name="scatter",
    )(
        counts,
        info[2].astype(jnp.int32),
        info[3].astype(jnp.int32),
        info[0],
        info[1],
        incoming,
    )

    def move(x, da, db):
        pairs = []
        for i in range(lat_total):
            for j in range(lon_total):
                if 0 <= i + da < lat_total:
                    pairs.append(
                        (i * lon_total + j, (i + da) * lon_total + (j + db) % lon_total)
                    )
        return lax.ppermute(x, axes, pairs)

    inset = before - 1
    far = inset + cols - 2
    halo = [
        move(up_s, -1, 0),
        move(down_s, 1, 0),
        move(left_s, 0, -1),
        move(right_s, 0, 1),
        move(up_s[:, :up], -1, -1),
        move(up_s[:, far : far + down], -1, 1),
        move(down_s[:, :up], 1, -1),
        move(down_s[:, far : far + down], 1, 1),
    ]
    edge = jnp.stack([lax.axis_index("lat"), lat_total]).astype(jnp.int32)
    kernel_t = conv_weight.transpose(0, 1, 3, 2).reshape(3, 3 * channels, channels)
    input_grad, part = pl.pallas_call(
        conv_kernel,
        out_shape=[
            jax.ShapeDtypeStruct((tile_lat, tile_lon, channels), bf16),
            jax.ShapeDtypeStruct((3, 3, channels, channels), bf16),
        ],
        in_specs=[smem] + [vmem] * 11,
        out_specs=[vmem] * 2,
        scratch_shapes=[
            pltpu.VMEM((rows, -(-cols // 8) * 8, channels), f32),
            pltpu.VMEM((rows * tile_lon, 3 * channels), bf16),
            pltpu.VMEM((channels, (rows + 2) * tile_lon), bf16),
            pltpu.VMEM((3 * channels, 3 * channels), f32),
        ],
        compiler_params=pltpu.CompilerParams(vmem_limit_bytes=60 * 2**20),
        name="conv",
    )(edge, own, *halo, features, kernel_t)
    pieces = part.reshape(device_total, -1, channels)
    pieces = lax.all_to_all(pieces, axes, split_axis=0, concat_axis=0, tiled=True)
    mine = jnp.sum(pieces.astype(f32), axis=0).astype(bf16)
    spread = jnp.broadcast_to(mine[None], (device_total,) + mine.shape)
    spread = lax.all_to_all(spread, axes, split_axis=0, concat_axis=0, tiled=True)
    weight_grad = spread.reshape(3, 3, channels, channels).astype(f32)
    return input_grad, weight_grad


def solution(mesh):
    placed = (
        P(("lat", "lon"), None),
        P(("lat", "lon"), None),
        P(("lat", "lon")),
        P(("lat", "lon")),
        P(("lat", "lon"), None),
        P(("lat", "lon")),
        P("lat", "lon", None),
        P(),
    )
    return jax.shard_map(
        shards, mesh=mesh, in_specs=placed, out_specs=(P("lat", "lon", None), P()), check_vma=False
    )
```

```python
import functools
import math

import jax
import jax.numpy as jnp
from jax import lax
from jax.experimental import pallas as pl
from jax.experimental.pallas import tpu as pltpu
from jax.sharding import PartitionSpec as P

rbf_scale = 1.5
taps = 8
before = 3
after = taps - 1 - before
geom_rows = 8
f32 = jnp.float32
bf16 = jnp.bfloat16


def pack_kernel(capacity, live_ref, rows_ref, owner_ref, lat_ref, lon_ref, pos_ref, out_ref):
    devices = out_ref.shape[0]
    row_total = rows_ref.shape[0]
    live = lax.broadcasted_iota(jnp.int32, (1, row_total), 1) < live_ref[0]
    owner = jnp.where(live, owner_ref[...], devices)
    match = lax.broadcasted_iota(jnp.int32, (devices, row_total), 0) == owner
    match = jnp.where(match, 1.0, 0.0)
    upper = lax.broadcasted_iota(jnp.int32, (row_total, row_total), 0) < lax.broadcasted_iota(
        jnp.int32, (row_total, row_total), 1
    )
    upper = jnp.where(upper, 1.0, 0.0).astype(bf16)
    earlier = jnp.dot(match.astype(bf16), upper, preferred_element_type=f32)
    rank = jnp.sum(earlier * match, axis=0, keepdims=True).astype(jnp.int32)
    slot = owner * capacity + rank
    geometry = jnp.concatenate(
        [
            pos_ref[...].astype(f32),
            lat_ref[...].astype(f32),
            lon_ref[...].astype(f32),
            jnp.where(live, 1.0, 0.0),
            jnp.zeros((geom_rows - 5, row_total), f32),
        ],
        axis=0,
    ).astype(bf16)
    group = max(1, min(devices, 256 // capacity))
    line = lax.broadcasted_iota(jnp.int32, (group * capacity, row_total), 0)
    for first in range(0, devices, group):
        hit = jnp.where(line == slot - first * capacity, 1.0, 0.0).astype(bf16)
        placed = jnp.dot(hit, rows_ref[...], preferred_element_type=f32).astype(bf16)
        info = lax.dot_general(
            geometry, hit, (((1,), (1,)), ((), ())), preferred_element_type=f32
        ).astype(bf16)
        for i in range(group):
            out_ref[first + i, 0:capacity, :] = placed[i * capacity : (i + 1) * capacity]
            out_ref[first + i, capacity : capacity + geom_rows, 0:capacity] = info[
                :, i * capacity : (i + 1) * capacity
            ]


def scatter_kernel(
    capacity,
    lanes,
    count_ref,
    lat_ref,
    lon_ref,
    fa_ref,
    fb_ref,
    msg_ref,
    own_ref,
    up_ref,
    down_ref,
    left_ref,
    right_ref,
    ul_ref,
    ur_ref,
    dl_ref,
    dr_ref,
    canvas,
    block,
):
    sources = msg_ref.shape[0]
    rows, cols = own_ref.shape[0], own_ref.shape[1]
    tall = canvas.shape[1]
    inv = 1.0 / (2.0 * rbf_scale * rbf_scale)

    def clear(i, _):
        for j in range(lanes):
            canvas[j, i] = jnp.zeros(canvas.shape[2:], f32)
        return 0

    lax.fori_loop(0, tall, clear, 0)
    line = lax.broadcasted_iota(jnp.int32, (taps, canvas.shape[3]), 0).astype(f32) - before
    level = [math.exp(-((a - before) ** 2 - before**2) * inv) for a in range(taps)]

    def source(src, _):
        block[...] = msg_ref[src, 0:capacity, :].astype(f32)

        def step(i, _):
            terms = []
            for j in range(lanes):
                s = i * lanes + j
                at = src * capacity + s
                fa = fa_ref[at]
                d = line - fb_ref[at]
                t = jnp.exp(-(d * d + (before + fa) * (before + fa)) * inv) * block[pl.ds(s, 1), :]
                g = jnp.exp(jnp.full(t.shape, 2.0 * inv, f32) * fa)
                terms.append((lat_ref[at], lon_ref[at], t, g))
            sums = []
            for j, (r, c, t, g) in enumerate(terms):
                for a in range(taps):
                    sums.append(canvas[j, r + a, pl.ds(c, taps), :] + t * level[a])
                    t = t * g
            for j, (r, c, _, _) in enumerate(terms):
                for a in range(taps):
                    canvas[j, r + a, pl.ds(c, taps), :] = sums[j * taps + a]
            return 0

        lax.fori_loop(0, (count_ref[src] + lanes - 1) // lanes, step, 0)
        return 0

    lax.fori_loop(0, sources, source, 0)
    up, down = before + 1, after + 1
    inset = before - 1

    def total(i):
        whole = canvas[0, i]
        for j in range(1, lanes):
            whole = whole + canvas[j, i]
        canvas[0, i] = whole

    def finish(i, _):
        total(i)
        return 0

    lax.fori_loop(0, tall, finish, 0)

    def emit(i, _):
        own_ref[i] = canvas[0, i + inset, inset : inset + cols, :].astype(bf16)
        left_ref[i] = canvas[0, i + inset, 0:up, :].astype(bf16)
        right_ref[i] = canvas[0, i + inset, inset + cols - 2 : inset + cols - 2 + down, :].astype(bf16)
        return 0

    lax.fori_loop(0, rows, emit, 0)
    spans = ((0, up), (inset, cols), (inset + cols - 2, down))
    for count, first, refs in (
        (up, 0, (ul_ref, up_ref, ur_ref)),
        (down, inset + rows - 2, (dl_ref, down_ref, dr_ref)),
    ):
        for i in range(count):
            for (start, width), ref in zip(spans, refs):
                ref[i] = canvas[0, first + i, start : start + width, :].astype(bf16)


def conv_kernel(
    lat_total,
    lon_total,
    own_ref,
    *refs,
):
    strips, (feat_ref, weight_ref, ig_ref, wg_ref) = refs[:8], refs[8:12]
    landed = refs[12:20]
    (grid, windows, turned, total, flat, pieces, parts, mine, gathered) = refs[20:29]
    halo_send, halo_recv, part_send, part_recv, all_send, all_recv = refs[29:]
    rows, cols = own_ref.shape[0], own_ref.shape[1]
    tile_lat, tile_lon, channels = feat_ref.shape
    up, down = before + 1, after + 1
    devices = lat_total * lon_total
    lat, lon = lax.axis_index("lat"), lax.axis_index("lon")
    me = lat * lon_total + lon

    def place(peer):
        return (peer // lon_total, peer % lon_total)

    barrier = pltpu.get_barrier_semaphore()

    def greet(k, _):
        pl.semaphore_signal(
            barrier, inc=1, device_id=place((me + k) % devices), device_id_type=pl.DeviceIdType.MESH
        )
        return 0

    lax.fori_loop(1, devices, greet, 0)

    def fill(i, _):
        grid[i, 0:cols, :] = own_ref[i].astype(f32)
        return 0

    lax.fori_loop(0, rows, fill, 0)
    pl.semaphore_wait(barrier, devices - 1)

    ways = ((-1, 0), (1, 0), (0, -1), (0, 1), (-1, -1), (-1, 1), (1, -1), (1, 1))
    halos = []
    for w, (da, db) in enumerate(ways):
        copy = pltpu.make_async_remote_copy(
            src_ref=strips[w],
            dst_ref=landed[w],
            send_sem=halo_send.at[w],
            recv_sem=halo_recv.at[w],
            device_id=((lat + da + lat_total) % lat_total, (lon + db + lon_total) % lon_total),
            device_id_type=pl.DeviceIdType.MESH,
        )
        sends = (lat + da >= 0) & (lat + da < lat_total)
        takes = (lat - da >= 0) & (lat - da < lat_total)
        halos.append((copy, sends, takes))

    def when(da, cond, fn):
        if da == 0:
            fn()
        else:
            pl.when(cond)(fn)

    for (copy, sends, _), (da, _) in zip(halos, ways):
        when(da, sends, copy.start)

    turned[:, 0 : 2 * tile_lon] = jnp.zeros((channels, 2 * tile_lon), bf16)
    turned[:, rows * tile_lon : (rows + 2) * tile_lon] = jnp.zeros((channels, 2 * tile_lon), bf16)

    def turn(p, _):
        turned[:, pl.ds(pl.multiple_of((p + 2) * tile_lon, tile_lon), tile_lon)] = feat_ref[p].T
        return 0

    lax.fori_loop(0, tile_lat, turn, 0)
    total[...] = jnp.zeros_like(total)

    for (copy, _, takes), (da, db), ref in zip(halos, ways, landed):

        def take(copy=copy, da=da, db=db, ref=ref):
            copy.wait_recv()
            high = {-1: rows - up, 0: 0, 1: 0}[da]
            count = {-1: up, 0: rows, 1: down}[da]
            left = {-1: cols - up, 0: 0, 1: 0}[db]
            width = {-1: up, 0: cols, 1: down}[db]

            def add(i, _):
                grid[high + i, left : left + width, :] += ref[i].astype(f32)
                return 0

            lax.fori_loop(0, count, add, 0)

        when(da, takes, take)

    @pl.when(lat == 0)
    def _():
        grid[0] = jnp.zeros(grid.shape[1:], f32)

    @pl.when(lat == lat_total - 1)
    def _():
        grid[rows - 1] = jnp.zeros(grid.shape[1:], f32)

    def shift(i, _):
        at = pl.ds(pl.multiple_of(i * tile_lon, tile_lon), tile_lon)
        for b in range(3):
            windows[at, b * channels : (b + 1) * channels] = grid[
                i, 2 - b : 2 - b + tile_lon, :
            ].astype(bf16)
        return 0

    lax.fori_loop(0, rows, shift, 0)
    step = next(n for n in (11, 6, 3, 2, 1) if rows % n == 0)
    depth = step * tile_lon

    def weigh(k, _):
        start = k * depth
        lhs = jnp.concatenate(
            [
                turned[:, pl.ds(pl.multiple_of(start + a * tile_lon, tile_lon), depth)]
                for a in range(3)
            ],
            axis=0,
        )
        rhs = windows[pl.ds(pl.multiple_of(start, tile_lon), depth), :]
        total[...] += jnp.dot(lhs, rhs, preferred_element_type=f32)
        return 0

    lax.fori_loop(0, rows // step, weigh, 0)
    for a in range(3):
        for b in range(3):
            at = (a * 3 + b) * channels
            flat[at : at + channels, :] = total[
                a * channels : (a + 1) * channels, b * channels : (b + 1) * channels
            ]
    share = pieces.shape[1]

    def cut(d, _):
        pieces[d] = flat[pl.ds(d * share, share), :].astype(bf16)
        return 0

    lax.fori_loop(0, devices, cut, 0)
    part = math.gcd(tile_lat, 8)
    strides = tile_lat // part
    half = strides // 2

    def apply(k, _):
        acc = jnp.zeros((part * tile_lon, channels), f32)
        for a in range(3):
            start = pl.multiple_of((k * part + 2 - a) * tile_lon, tile_lon)
            acc = acc + jnp.dot(
                windows[pl.ds(start, part * tile_lon), :], weight_ref[a], preferred_element_type=f32
            )
        ig_ref[pl.ds(k * part, part)] = acc.reshape(part, tile_lon, channels).astype(bf16)
        return 0

    def scattered(peer, slot):
        return pltpu.make_async_remote_copy(
            src_ref=pieces.at[peer],
            dst_ref=parts.at[slot],
            send_sem=part_send.at[peer],
            recv_sem=part_recv.at[slot],
            device_id=place(peer),
            device_id_type=pl.DeviceIdType.MESH,
        )

    def shared(peer, slot):
        return pltpu.make_async_remote_copy(
            src_ref=mine,
            dst_ref=gathered.at[slot],
            send_sem=all_send.at[peer],
            recv_sem=all_recv.at[slot],
            device_id=place(peer),
            device_id_type=pl.DeviceIdType.MESH,
        )

    def each(fn):
        def body(k, _):
            fn((me + k) % devices)
            return 0

        lax.fori_loop(1, devices, body, 0)

    each(lambda peer: scattered(peer, me).start())
    lax.fori_loop(0, half, apply, 0)
    each(lambda peer: scattered(peer, peer).wait_recv())
    parts[me] = pieces[me]

    def gather_sum(d, acc):
        return acc + parts[d].astype(f32)

    mine[...] = lax.fori_loop(
        0, devices, gather_sum, jnp.zeros((share, channels), f32)
    ).astype(bf16)
    each(lambda peer: shared(peer, me).start())
    lax.fori_loop(half, strides, apply, 0)
    each(lambda peer: shared(peer, peer).wait_recv())
    gathered[me] = mine[...]

    def spill(d, _):
        wg_ref[pl.ds(d * share, share), :] = gathered[d].astype(f32)
        return 0

    lax.fori_loop(0, devices, spill, 0)
    for (copy, sends, _), (da, _) in zip(halos, ways):
        when(da, sends, copy.wait_send)
    each(lambda peer: scattered(peer, me).wait_send())
    each(lambda peer: shared(peer, me).wait_send())


def shards(grad_rows, owner, lat_offset, lon_offset, position, live_count, features, conv_weight):
    lat_total = lax.axis_size("lat")
    lon_total = lax.axis_size("lon")
    device_total = lat_total * lon_total
    row_total, channels = grad_rows.shape
    tile_lat, tile_lon = features.shape[:2]
    capacity = max(2, 2 * row_total // device_total)
    smem = pl.BlockSpec(memory_space=pltpu.SMEM)
    vmem = pl.BlockSpec(memory_space=pltpu.VMEM)
    axes = ("lat", "lon")

    outgoing = pl.pallas_call(
        functools.partial(pack_kernel, capacity),
        out_shape=jax.ShapeDtypeStruct((device_total, capacity + geom_rows, channels), bf16),
        in_specs=[smem] + [vmem] * 5,
        out_specs=vmem,
        name="pack",
    )(
        live_count,
        grad_rows,
        owner.reshape(1, row_total),
        lat_offset.reshape(1, row_total),
        lon_offset.reshape(1, row_total),
        position.T,
    )
    incoming = lax.all_to_all(outgoing, axes, split_axis=0, concat_axis=0, tiled=True)
    info = incoming[:, capacity : capacity + 5, :capacity].astype(f32).transpose(1, 0, 2)
    counts = jnp.sum(info[4], axis=1).astype(jnp.int32)
    info = info.reshape(5, -1)

    rows, cols = tile_lat + 2, tile_lon + 2
    tall = tile_lat + taps - 1
    wide = -(-(tile_lon + taps - 1) // 8) * 8
    up, down = before + 1, after + 1
    lanes = math.gcd(capacity, 4)
    strip_shapes = [
        (up, cols),
        (down, cols),
        (rows, up),
        (rows, down),
        (up, up),
        (up, down),
        (down, up),
        (down, down),
    ]
    own, *strips = pl.pallas_call(
        functools.partial(scatter_kernel, capacity, lanes),
        out_shape=[
            jax.ShapeDtypeStruct(shape + (channels,), bf16)
            for shape in [(rows, cols)] + strip_shapes
        ],
        in_specs=[smem] * 5 + [vmem],
        out_specs=[vmem] * 9,
        scratch_shapes=[
            pltpu.VMEM((lanes, tall, wide, channels), f32),
            pltpu.VMEM((capacity, channels), f32),
        ],
        compiler_params=pltpu.CompilerParams(vmem_limit_bytes=60 * 2**20),
        name="scatter",
    )(
        counts,
        info[2].astype(jnp.int32),
        info[3].astype(jnp.int32),
        info[0],
        info[1],
        incoming,
    )
    kernel_t = conv_weight.transpose(0, 1, 3, 2).reshape(3, 3 * channels, channels)
    flat_rows = 9 * channels
    share = flat_rows // device_total
    ring = pltpu.VMEM((device_total, share, channels), bf16)
    input_grad, weight_grad = pl.pallas_call(
        functools.partial(conv_kernel, lat_total, lon_total),
        out_shape=[
            jax.ShapeDtypeStruct((tile_lat, tile_lon, channels), bf16),
            jax.ShapeDtypeStruct((flat_rows, channels), f32),
        ],
        in_specs=[vmem] * 11,
        out_specs=[vmem] * 2,
        scratch_shapes=[pltpu.VMEM(shape + (channels,), bf16) for shape in strip_shapes]
        + [
            pltpu.VMEM((rows, -(-cols // 8) * 8, channels), f32),
            pltpu.VMEM((rows * tile_lon, 3 * channels), bf16),
            pltpu.VMEM((channels, (rows + 2) * tile_lon), bf16),
            pltpu.VMEM((3 * channels, 3 * channels), f32),
            pltpu.VMEM((flat_rows, channels), f32),
            ring,
            ring,
            pltpu.VMEM((share, channels), bf16),
            ring,
            pltpu.SemaphoreType.DMA((8,)),
            pltpu.SemaphoreType.DMA((8,)),
            pltpu.SemaphoreType.DMA((device_total,)),
            pltpu.SemaphoreType.DMA((device_total,)),
            pltpu.SemaphoreType.DMA((device_total,)),
            pltpu.SemaphoreType.DMA((device_total,)),
        ],
        compiler_params=pltpu.CompilerParams(
            vmem_limit_bytes=60 * 2**20, collective_id=0, has_side_effects=True
        ),
        name="conv",
    )(own, *strips, features, kernel_t)
    return input_grad, weight_grad.reshape(3, 3, channels, channels)


def solution(mesh):
    placed = (
        P(("lat", "lon"), None),
        P(("lat", "lon"), None),
        P(("lat", "lon")),
        P(("lat", "lon")),
        P(("lat", "lon"), None),
        P(("lat", "lon")),
        P("lat", "lon", None),
        P(),
    )
    return jax.shard_map(
        shards, mesh=mesh, in_specs=placed, out_specs=(P("lat", "lon", None), P()), check_vma=False
    )
```

```python
import functools
import math

import jax
import jax.numpy as jnp
from jax import lax
from jax.experimental import pallas as pl
from jax.experimental.pallas import tpu as pltpu
from jax.sharding import PartitionSpec as P

rbf_scale = 1.5
taps = 8
before = 3
after = taps - 1 - before
geom_rows = 8
f32 = jnp.float32
bf16 = jnp.bfloat16


def pack_kernel(
    capacity,
    lat_total,
    lon_total,
    live_ref,
    rows_ref,
    owner_ref,
    lat_ref,
    lon_ref,
    pos_ref,
    out_ref,
    held,
    tally,
    send_sem,
    recv_sem,
):
    devices = out_ref.shape[0]
    row_total, channels = rows_ref.shape
    me = lax.axis_index("lat") * lon_total + lax.axis_index("lon")

    def place(peer):
        return (peer // lon_total, peer % lon_total)

    barrier = pltpu.get_barrier_semaphore()

    def greet(k, _):
        pl.semaphore_signal(
            barrier, inc=1, device_id=place((me + k) % devices), device_id_type=pl.DeviceIdType.MESH
        )
        return 0

    lax.fori_loop(1, devices, greet, 0)
    live = lax.broadcasted_iota(jnp.int32, (1, row_total), 1) < live_ref[0]
    owner = jnp.where(live, owner_ref[...], devices)
    match = lax.broadcasted_iota(jnp.int32, (devices, row_total), 0) == owner
    match = jnp.where(match, 1.0, 0.0)
    tally[...] = jnp.broadcast_to(jnp.sum(match, axis=1, keepdims=True), tally.shape)
    upper = lax.broadcasted_iota(jnp.int32, (row_total, row_total), 0) < lax.broadcasted_iota(
        jnp.int32, (row_total, row_total), 1
    )
    upper = jnp.where(upper, 1.0, 0.0).astype(bf16)
    earlier = jnp.dot(match.astype(bf16), upper, preferred_element_type=f32)
    rank = jnp.sum(earlier * match, axis=0, keepdims=True).astype(jnp.int32)
    slot = owner * capacity + rank
    geometry = jnp.concatenate(
        [
            pos_ref[...].astype(f32),
            lat_ref[...].astype(f32),
            lon_ref[...].astype(f32),
            jnp.zeros((geom_rows - 4, row_total), f32),
        ],
        axis=0,
    ).astype(bf16)
    group = math.gcd(devices, max(1, 256 // capacity))
    groups = devices // group
    line = lax.broadcasted_iota(jnp.int32, (group * capacity, row_total), 0)
    row_line = lax.broadcasted_iota(jnp.int32, (geom_rows, capacity), 0)

    def build(first):
        hit = jnp.where(line == slot - first * capacity, 1.0, 0.0).astype(bf16)
        placed = jnp.dot(hit, rows_ref[...], preferred_element_type=f32).astype(bf16)
        info = lax.dot_general(
            geometry, hit, (((1,), (1,)), ((), ())), preferred_element_type=f32
        )
        for i in range(group):
            held[first + i, 0:capacity, :] = placed[i * capacity : (i + 1) * capacity]
            held[first + i, capacity : capacity + geom_rows, 0:capacity] = jnp.where(
                row_line == 4,
                tally[pl.ds(first + i, 1), 0:capacity],
                info[:, i * capacity : (i + 1) * capacity],
            ).astype(bf16)

    def copy_to(peer, slot_at):
        return pltpu.make_async_remote_copy(
            src_ref=held.at[peer],
            dst_ref=out_ref.at[slot_at],
            send_sem=send_sem.at[peer],
            recv_sem=recv_sem.at[slot_at],
            device_id=place(peer),
            device_id_type=pl.DeviceIdType.MESH,
        )

    def send(first):
        for i in range(group):
            peer = first + i

            @pl.when(peer != me)
            def _():
                copy_to(peer, me).start()

    odd = groups // 2

    def first_of(k):
        ahead = jnp.where(k < odd, 2 * k + 1, 2 * (k - odd))
        return ((me // group + ahead) % groups) * group

    build(first_of(0))
    pl.semaphore_wait(barrier, devices - 1)

    def work(k, _):
        build(first_of(k))
        send(first_of(k - 1))
        return 0

    lax.fori_loop(1, groups, work, 0)
    send(first_of(groups - 1))
    out_ref[me] = held[me]

    def each(fn):
        def body(k, _):
            fn((me + k) % devices)
            return 0

        lax.fori_loop(1, devices, body, 0)

    each(lambda peer: copy_to(peer, peer).wait_recv())
    each(lambda peer: copy_to(peer, me).wait_send())


def scatter_kernel(
    capacity,
    lanes,
    info_ref,
    msg_ref,
    own_ref,
    up_ref,
    down_ref,
    left_ref,
    right_ref,
    ul_ref,
    ur_ref,
    dl_ref,
    dr_ref,
    canvas,
    block,
):
    sources = msg_ref.shape[0]
    slots = sources * capacity
    rows, cols = own_ref.shape[0], own_ref.shape[1]
    tall = canvas.shape[1]
    inv = 1.0 / (2.0 * rbf_scale * rbf_scale)

    def clear(i, _):
        for j in range(lanes):
            canvas[j, i] = jnp.zeros(canvas.shape[2:], f32)
        return 0

    lax.fori_loop(0, tall, clear, 0)
    line = lax.broadcasted_iota(jnp.int32, (taps, canvas.shape[3]), 0).astype(f32) - before
    level = [math.exp(-((a - before) ** 2 - before**2) * inv) for a in range(taps)]

    def source(src, _):
        block[...] = msg_ref[src, 0:capacity, :].astype(f32)

        def prepare(i):
            terms = []
            for j in range(lanes):
                s = i * lanes + j
                at = src * capacity + s
                fa, fb = info_ref[at], info_ref[at + slots]
                d = line - fb
                t = jnp.exp(-(d * d + (before + fa) * (before + fa)) * inv) * block[pl.ds(s, 1), :]
                g = jnp.exp(jnp.full(t.shape, 2.0 * inv, f32) * fa)
                r = info_ref[at + 2 * slots].astype(jnp.int32)
                c = info_ref[at + 3 * slots].astype(jnp.int32)
                terms.append((r, c, t, g))
            return tuple(terms)

        trips = (info_ref[4 * slots + src * capacity].astype(jnp.int32) + lanes - 1) // lanes

        def step(i, terms):
            ahead = prepare(jnp.minimum(i + 1, trips - 1))
            sums = []
            for j, (r, c, t, g) in enumerate(terms):
                for a in range(taps):
                    sums.append(canvas[j, r + a, pl.ds(c, taps), :] + t * level[a])
                    t = t * g
            for j, (r, c, _, _) in enumerate(terms):
                for a in range(taps):
                    canvas[j, r + a, pl.ds(c, taps), :] = sums[j * taps + a]
            return ahead

        lax.fori_loop(0, trips, step, prepare(0))
        return 0

    lax.fori_loop(0, sources, source, 0)
    up, down = before + 1, after + 1
    inset = before - 1

    def total(i):
        whole = canvas[0, i]
        for j in range(1, lanes):
            whole = whole + canvas[j, i]
        canvas[0, i] = whole

    def finish(i, _):
        total(i)
        return 0

    lax.fori_loop(0, tall, finish, 0)

    def emit(i, _):
        own_ref[i] = canvas[0, i + inset, inset : inset + cols, :].astype(bf16)
        left_ref[i] = canvas[0, i + inset, 0:up, :].astype(bf16)
        right_ref[i] = canvas[0, i + inset, inset + cols - 2 : inset + cols - 2 + down, :].astype(bf16)
        return 0

    lax.fori_loop(0, rows, emit, 0)
    spans = ((0, up), (inset, cols), (inset + cols - 2, down))
    for count, first, refs in (
        (up, 0, (ul_ref, up_ref, ur_ref)),
        (down, inset + rows - 2, (dl_ref, down_ref, dr_ref)),
    ):
        for i in range(count):
            for (start, width), ref in zip(spans, refs):
                ref[i] = canvas[0, first + i, start : start + width, :].astype(bf16)


def conv_kernel(
    lat_total,
    lon_total,
    own_ref,
    *refs,
):
    strips, (feat_ref, weight_ref, ig_ref, wg_ref) = refs[:8], refs[8:12]
    landed = refs[12:20]
    (grid, windows, turned, total, flat, pieces, parts, mine, gathered) = refs[20:29]
    halo_send, halo_recv, part_send, part_recv, all_send, all_recv = refs[29:]
    rows, cols = own_ref.shape[0], own_ref.shape[1]
    tile_lat, tile_lon, channels = feat_ref.shape
    up, down = before + 1, after + 1
    devices = lat_total * lon_total
    lat, lon = lax.axis_index("lat"), lax.axis_index("lon")
    me = lat * lon_total + lon

    def place(peer):
        return (peer // lon_total, peer % lon_total)

    barrier = pltpu.get_barrier_semaphore()

    def greet(k, _):
        pl.semaphore_signal(
            barrier, inc=1, device_id=place((me + k) % devices), device_id_type=pl.DeviceIdType.MESH
        )
        return 0

    lax.fori_loop(1, devices, greet, 0)

    def fill(i, _):
        grid[i, 0:cols, :] = own_ref[i].astype(f32)
        return 0

    lax.fori_loop(0, rows, fill, 0)
    pl.semaphore_wait(barrier, devices - 1)

    ways = ((-1, 0), (1, 0), (0, -1), (0, 1), (-1, -1), (-1, 1), (1, -1), (1, 1))
    halos = []
    for w, (da, db) in enumerate(ways):
        copy = pltpu.make_async_remote_copy(
            src_ref=strips[w],
            dst_ref=landed[w],
            send_sem=halo_send.at[w],
            recv_sem=halo_recv.at[w],
            device_id=((lat + da + lat_total) % lat_total, (lon + db + lon_total) % lon_total),
            device_id_type=pl.DeviceIdType.MESH,
        )
        sends = (lat + da >= 0) & (lat + da < lat_total)
        takes = (lat - da >= 0) & (lat - da < lat_total)
        halos.append((copy, sends, takes))

    def when(da, cond, fn):
        if da == 0:
            fn()
        else:
            pl.when(cond)(fn)

    for (copy, sends, _), (da, _) in zip(halos, ways):
        when(da, sends, copy.start)

    turned[:, 0 : 2 * tile_lon] = jnp.zeros((channels, 2 * tile_lon), bf16)
    turned[:, rows * tile_lon : (rows + 2) * tile_lon] = jnp.zeros((channels, 2 * tile_lon), bf16)

    def turn(p, _):
        turned[:, pl.ds(pl.multiple_of((p + 2) * tile_lon, tile_lon), tile_lon)] = feat_ref[p].T
        return 0

    lax.fori_loop(0, tile_lat, turn, 0)
    total[...] = jnp.zeros_like(total)

    for (copy, _, takes), (da, db), ref in zip(halos, ways, landed):

        def take(copy=copy, da=da, db=db, ref=ref):
            copy.wait_recv()
            high = {-1: rows - up, 0: 0, 1: 0}[da]
            count = {-1: up, 0: rows, 1: down}[da]
            left = {-1: cols - up, 0: 0, 1: 0}[db]
            width = {-1: up, 0: cols, 1: down}[db]

            def add(i, _):
                grid[high + i, left : left + width, :] += ref[i].astype(f32)
                return 0

            lax.fori_loop(0, count, add, 0)

        when(da, takes, take)

    @pl.when(lat == 0)
    def _():
        grid[0] = jnp.zeros(grid.shape[1:], f32)

    @pl.when(lat == lat_total - 1)
    def _():
        grid[rows - 1] = jnp.zeros(grid.shape[1:], f32)

    def shift(i, _):
        at = pl.ds(pl.multiple_of(i * tile_lon, tile_lon), tile_lon)
        for b in range(3):
            windows[at, b * channels : (b + 1) * channels] = grid[
                i, 2 - b : 2 - b + tile_lon, :
            ].astype(bf16)
        return 0

    lax.fori_loop(0, rows, shift, 0)
    step = next(n for n in (11, 6, 3, 2, 1) if rows % n == 0)
    depth = step * tile_lon

    def weigh(k, _):
        start = k * depth
        lhs = jnp.concatenate(
            [
                turned[:, pl.ds(pl.multiple_of(start + a * tile_lon, tile_lon), depth)]
                for a in range(3)
            ],
            axis=0,
        )
        rhs = windows[pl.ds(pl.multiple_of(start, tile_lon), depth), :]
        total[...] += jnp.dot(lhs, rhs, preferred_element_type=f32)
        return 0

    lax.fori_loop(0, rows // step, weigh, 0)
    for a in range(3):
        for b in range(3):
            at = (a * 3 + b) * channels
            flat[at : at + channels, :] = total[
                a * channels : (a + 1) * channels, b * channels : (b + 1) * channels
            ]
    share = pieces.shape[1]

    def cut(d, _):
        pieces[d] = flat[pl.ds(d * share, share), :].astype(bf16)
        return 0

    lax.fori_loop(0, devices, cut, 0)
    part = math.gcd(tile_lat // 2, 8)
    strides = tile_lat // 2 // part
    half = strides // 2

    def apply(k, _):
        lhs = jnp.concatenate(
            [
                jnp.concatenate(
                    [
                        windows[
                            pl.ds(
                                pl.multiple_of((2 * (k * part + j) + r) * tile_lon, tile_lon),
                                tile_lon,
                            ),
                            :,
                        ]
                        for r in range(4)
                    ],
                    axis=1,
                )
                for j in range(part)
            ],
            axis=0,
        )
        acc = jnp.dot(lhs, weight_ref[...], preferred_element_type=f32).astype(bf16)
        for j in range(part):
            for r in range(2):
                ig_ref[2 * (k * part + j) + r] = acc[
                    j * tile_lon : (j + 1) * tile_lon, r * channels : (r + 1) * channels
                ]
        return 0

    def scattered(peer, slot):
        return pltpu.make_async_remote_copy(
            src_ref=pieces.at[peer],
            dst_ref=parts.at[slot],
            send_sem=part_send.at[peer],
            recv_sem=part_recv.at[slot],
            device_id=place(peer),
            device_id_type=pl.DeviceIdType.MESH,
        )

    def shared(peer, slot):
        return pltpu.make_async_remote_copy(
            src_ref=mine,
            dst_ref=gathered.at[slot],
            send_sem=all_send.at[peer],
            recv_sem=all_recv.at[slot],
            device_id=place(peer),
            device_id_type=pl.DeviceIdType.MESH,
        )

    def each(fn):
        def body(k, _):
            fn((me + k) % devices)
            return 0

        lax.fori_loop(1, devices, body, 0)

    each(lambda peer: scattered(peer, me).start())
    lax.fori_loop(0, half, apply, 0)
    each(lambda peer: scattered(peer, peer).wait_recv())
    parts[me] = pieces[me]

    def gather_sum(d, acc):
        return acc + parts[d].astype(f32)

    mine[...] = lax.fori_loop(
        0, devices, gather_sum, jnp.zeros((share, channels), f32)
    ).astype(bf16)
    each(lambda peer: shared(peer, me).start())
    lax.fori_loop(half, strides, apply, 0)
    each(lambda peer: shared(peer, peer).wait_recv())
    gathered[me] = mine[...]

    def spill(d, _):
        wg_ref[pl.ds(d * share, share), :] = gathered[d].astype(f32)
        return 0

    lax.fori_loop(0, devices, spill, 0)
    for (copy, sends, _), (da, _) in zip(halos, ways):
        when(da, sends, copy.wait_send)
    each(lambda peer: scattered(peer, me).wait_send())
    each(lambda peer: shared(peer, me).wait_send())


def shards(grad_rows, owner, lat_offset, lon_offset, position, live_count, features, conv_weight):
    lat_total = lax.axis_size("lat")
    lon_total = lax.axis_size("lon")
    device_total = lat_total * lon_total
    row_total, channels = grad_rows.shape
    tile_lat, tile_lon = features.shape[:2]
    capacity = max(2, 2 * row_total // device_total)
    smem = pl.BlockSpec(memory_space=pltpu.SMEM)
    vmem = pl.BlockSpec(memory_space=pltpu.VMEM)

    message = (device_total, capacity + geom_rows, channels)
    incoming = pl.pallas_call(
        functools.partial(pack_kernel, capacity, lat_total, lon_total),
        out_shape=jax.ShapeDtypeStruct(message, bf16),
        in_specs=[smem] + [vmem] * 5,
        out_specs=vmem,
        scratch_shapes=[
            pltpu.VMEM(message, bf16),
            pltpu.VMEM((device_total, channels), f32),
            pltpu.SemaphoreType.DMA((device_total,)),
            pltpu.SemaphoreType.DMA((device_total,)),
        ],
        compiler_params=pltpu.CompilerParams(
            vmem_limit_bytes=24 * 2**20, collective_id=1, has_side_effects=True
        ),
        name="pack",
    )(
        live_count,
        grad_rows,
        owner.reshape(1, row_total),
        lat_offset.reshape(1, row_total),
        lon_offset.reshape(1, row_total),
        position.T,
    )
    info = incoming[:, capacity : capacity + 5, :capacity].transpose(1, 0, 2).astype(f32)
    info = info.reshape(-1)

    rows, cols = tile_lat + 2, tile_lon + 2
    tall = tile_lat + taps - 1
    wide = -(-(tile_lon + taps - 1) // 8) * 8
    up, down = before + 1, after + 1
    lanes = math.gcd(capacity, 4)
    strip_shapes = [
        (up, cols),
        (down, cols),
        (rows, up),
        (rows, down),
        (up, up),
        (up, down),
        (down, up),
        (down, down),
    ]
    own, *strips = pl.pallas_call(
        functools.partial(scatter_kernel, capacity, lanes),
        out_shape=[
            jax.ShapeDtypeStruct(shape + (channels,), bf16)
            for shape in [(rows, cols)] + strip_shapes
        ],
        in_specs=[smem, vmem],
        out_specs=[vmem] * 9,
        scratch_shapes=[
            pltpu.VMEM((lanes, tall, wide, channels), f32),
            pltpu.VMEM((capacity, channels), f32),
        ],
        compiler_params=pltpu.CompilerParams(vmem_limit_bytes=32 * 2**20),
        name="scatter",
    )(
        info,
        incoming,
    )
    kernel_t = conv_weight.transpose(0, 1, 3, 2).reshape(3, 3 * channels, channels)
    none = jnp.zeros_like(kernel_t[0])
    kernel_t = jnp.concatenate(
        [
            jnp.concatenate([kernel_t[2], kernel_t[1], kernel_t[0], none], axis=0),
            jnp.concatenate([none, kernel_t[2], kernel_t[1], kernel_t[0]], axis=0),
        ],
        axis=1,
    )
    flat_rows = 9 * channels
    share = flat_rows // device_total
    ring = pltpu.VMEM((device_total, share, channels), bf16)
    input_grad, weight_grad = pl.pallas_call(
        functools.partial(conv_kernel, lat_total, lon_total),
        out_shape=[
            jax.ShapeDtypeStruct((tile_lat, tile_lon, channels), bf16),
            jax.ShapeDtypeStruct((flat_rows, channels), f32),
        ],
        in_specs=[vmem] * 11,
        out_specs=[vmem] * 2,
        scratch_shapes=[pltpu.VMEM(shape + (channels,), bf16) for shape in strip_shapes]
        + [
            pltpu.VMEM((rows, -(-cols // 8) * 8, channels), f32),
            pltpu.VMEM((rows * tile_lon, 3 * channels), bf16),
            pltpu.VMEM((channels, (rows + 2) * tile_lon), bf16),
            pltpu.VMEM((3 * channels, 3 * channels), f32),
            pltpu.VMEM((flat_rows, channels), f32),
            ring,
            ring,
            pltpu.VMEM((share, channels), bf16),
            ring,
            pltpu.SemaphoreType.DMA((8,)),
            pltpu.SemaphoreType.DMA((8,)),
            pltpu.SemaphoreType.DMA((device_total,)),
            pltpu.SemaphoreType.DMA((device_total,)),
            pltpu.SemaphoreType.DMA((device_total,)),
            pltpu.SemaphoreType.DMA((device_total,)),
        ],
        compiler_params=pltpu.CompilerParams(
            vmem_limit_bytes=36 * 2**20, collective_id=0, has_side_effects=True
        ),
        name="conv",
    )(own, *strips, features, kernel_t)
    return input_grad, weight_grad.reshape(3, 3, channels, channels)


def solution(mesh):
    placed = (
        P(("lat", "lon"), None),
        P(("lat", "lon"), None),
        P(("lat", "lon")),
        P(("lat", "lon")),
        P(("lat", "lon"), None),
        P(("lat", "lon")),
        P("lat", "lon", None),
        P(),
    )
    return jax.shard_map(
        shards, mesh=mesh, in_specs=placed, out_specs=(P("lat", "lon", None), P()), check_vma=False
    )
```

```python
import functools
import math

import jax
import jax.numpy as jnp
from jax import lax
from jax.experimental import pallas as pl
from jax.experimental.pallas import tpu as pltpu
from jax.sharding import PartitionSpec as P

rbf_scale = 1.5
taps = 8
before = 3
after = taps - 1 - before
geom_rows = 8
f32 = jnp.float32
bf16 = jnp.bfloat16


def pack_kernel(
    capacity,
    lat_total,
    lon_total,
    live_ref,
    rows_ref,
    owner_ref,
    lat_ref,
    lon_ref,
    pos_ref,
    out_ref,
    held,
    tally,
    send_sem,
    recv_sem,
):
    devices = out_ref.shape[0]
    row_total, channels = rows_ref.shape
    me = lax.axis_index("lat") * lon_total + lax.axis_index("lon")

    def place(peer):
        return (peer // lon_total, peer % lon_total)

    barrier = pltpu.get_barrier_semaphore()

    def greet(k, _):
        pl.semaphore_signal(
            barrier, inc=1, device_id=place((me + k) % devices), device_id_type=pl.DeviceIdType.MESH
        )
        return 0

    lax.fori_loop(1, devices, greet, 0)
    live = lax.broadcasted_iota(jnp.int32, (1, row_total), 1) < live_ref[0]
    owner = jnp.where(live, owner_ref[...], devices)
    match = lax.broadcasted_iota(jnp.int32, (devices, row_total), 0) == owner
    match = jnp.where(match, 1.0, 0.0)
    tally[...] = jnp.broadcast_to(jnp.sum(match, axis=1, keepdims=True), tally.shape)
    upper = lax.broadcasted_iota(jnp.int32, (row_total, row_total), 0) < lax.broadcasted_iota(
        jnp.int32, (row_total, row_total), 1
    )
    upper = jnp.where(upper, 1.0, 0.0).astype(bf16)
    earlier = jnp.dot(match.astype(bf16), upper, preferred_element_type=f32)
    rank = jnp.sum(earlier * match, axis=0, keepdims=True).astype(jnp.int32)
    slot = owner * capacity + rank
    geometry = jnp.concatenate(
        [
            pos_ref[...].astype(f32),
            lat_ref[...].astype(f32),
            lon_ref[...].astype(f32),
            jnp.zeros((geom_rows - 4, row_total), f32),
        ],
        axis=0,
    ).astype(bf16)
    group = math.gcd(devices, max(1, 256 // capacity))
    groups = devices // group
    line = lax.broadcasted_iota(jnp.int32, (group * capacity, row_total), 0)
    row_line = lax.broadcasted_iota(jnp.int32, (geom_rows, capacity), 0)

    def build(first):
        hit = jnp.where(line == slot - first * capacity, 1.0, 0.0).astype(bf16)
        placed = jnp.dot(hit, rows_ref[...], preferred_element_type=f32).astype(bf16)
        info = lax.dot_general(
            geometry, hit, (((1,), (1,)), ((), ())), preferred_element_type=f32
        )
        for i in range(group):
            held[first + i, 0:capacity, :] = placed[i * capacity : (i + 1) * capacity]
            held[first + i, capacity : capacity + geom_rows, 0:capacity] = jnp.where(
                row_line == 4,
                tally[pl.ds(first + i, 1), 0:capacity],
                info[:, i * capacity : (i + 1) * capacity],
            ).astype(bf16)

    def copy_to(peer, slot_at):
        return pltpu.make_async_remote_copy(
            src_ref=held.at[peer],
            dst_ref=out_ref.at[slot_at],
            send_sem=send_sem.at[peer],
            recv_sem=recv_sem.at[slot_at],
            device_id=place(peer),
            device_id_type=pl.DeviceIdType.MESH,
        )

    def send(first):
        for i in range(group):
            peer = first + i

            @pl.when(peer != me)
            def _():
                copy_to(peer, me).start()

    odd = groups // 2

    def first_of(k):
        ahead = jnp.where(k < odd, 2 * k + 1, 2 * (k - odd))
        return ((me // group + ahead) % groups) * group

    build(first_of(0))
    pl.semaphore_wait(barrier, devices - 1)

    def work(k, _):
        build(first_of(k))
        send(first_of(k - 1))
        return 0

    lax.fori_loop(1, groups, work, 0)
    send(first_of(groups - 1))
    out_ref[me] = held[me]

    def each(fn):
        def body(k, _):
            fn((me + k) % devices)
            return 0

        lax.fori_loop(1, devices, body, 0)

    each(lambda peer: copy_to(peer, peer).wait_recv())
    each(lambda peer: copy_to(peer, me).wait_send())


def scatter_kernel(
    capacity,
    lanes,
    info_ref,
    msg_ref,
    own_ref,
    up_ref,
    down_ref,
    left_ref,
    right_ref,
    ul_ref,
    ur_ref,
    dl_ref,
    dr_ref,
    canvas,
    block,
):
    sources = msg_ref.shape[0]
    slots = sources * capacity
    rows, cols = own_ref.shape[0], own_ref.shape[1]
    tall = canvas.shape[1]
    inv = 1.0 / (2.0 * rbf_scale * rbf_scale)

    def clear(i, _):
        for j in range(lanes):
            canvas[j, i] = jnp.zeros(canvas.shape[2:], f32)
        return 0

    lax.fori_loop(0, tall, clear, 0)
    line = lax.broadcasted_iota(jnp.int32, (taps, canvas.shape[3]), 0).astype(f32) - before
    level = [math.exp(-((a - before) ** 2 - before**2) * inv) for a in range(taps)]

    def source(src, _):
        block[...] = msg_ref[src, 0:capacity, :].astype(f32)

        def prepare(i):
            terms = []
            for j in range(lanes):
                s = i * lanes + j
                at = src * capacity + s
                fa, fb = info_ref[at], info_ref[at + slots]
                d = line - fb
                t = jnp.exp(-(d * d + (before + fa) * (before + fa)) * inv) * block[pl.ds(s, 1), :]
                g = jnp.exp(jnp.full(t.shape, 2.0 * inv, f32) * fa)
                r = info_ref[at + 2 * slots].astype(jnp.int32)
                c = info_ref[at + 3 * slots].astype(jnp.int32)
                terms.append((r, c, t, g))
            return tuple(terms)

        trips = (info_ref[4 * slots + src * capacity].astype(jnp.int32) + lanes - 1) // lanes

        def step(i, terms):
            ahead = prepare(jnp.minimum(i + 1, trips - 1))
            sums = []
            for j, (r, c, t, g) in enumerate(terms):
                for a in range(taps):
                    sums.append(canvas[j, r + a, pl.ds(c, taps), :] + t * level[a])
                    t = t * g
            for j, (r, c, _, _) in enumerate(terms):
                for a in range(taps):
                    canvas[j, r + a, pl.ds(c, taps), :] = sums[j * taps + a]
            return ahead

        lax.fori_loop(0, trips, step, prepare(0))
        return 0

    lax.fori_loop(0, sources, source, 0)
    up, down = before + 1, after + 1
    inset = before - 1

    def total(i):
        whole = canvas[0, i]
        for j in range(1, lanes):
            whole = whole + canvas[j, i]
        canvas[0, i] = whole

    def finish(i, _):
        total(i)
        return 0

    lax.fori_loop(0, tall, finish, 0)

    def emit(i, _):
        own_ref[i] = canvas[0, i + inset, inset : inset + cols, :].astype(bf16)
        left_ref[i] = canvas[0, i + inset, 0:up, :].astype(bf16)
        right_ref[i] = canvas[0, i + inset, inset + cols - 2 : inset + cols - 2 + down, :].astype(bf16)
        return 0

    lax.fori_loop(0, rows, emit, 0)
    spans = ((0, up), (inset, cols), (inset + cols - 2, down))
    for count, first, refs in (
        (up, 0, (ul_ref, up_ref, ur_ref)),
        (down, inset + rows - 2, (dl_ref, down_ref, dr_ref)),
    ):
        for i in range(count):
            for (start, width), ref in zip(spans, refs):
                ref[i] = canvas[0, first + i, start : start + width, :].astype(bf16)


def conv_kernel(
    lat_total,
    lon_total,
    own_ref,
    *refs,
):
    strips, (feat_ref, weight_ref, ig_ref, wg_ref) = refs[:8], refs[8:12]
    landed = refs[12:20]
    (grid, windows, turned, total, flat, mixer, pieces, twin, parts, mine, gathered) = refs[20:31]
    halo_send, halo_recv, pair_send, pair_recv, part_send, part_recv, all_send, all_recv = refs[31:]
    rows, cols = own_ref.shape[0], own_ref.shape[1]
    tile_lat, tile_lon, channels = feat_ref.shape
    up, down = before + 1, after + 1
    devices = lat_total * lon_total
    lat, lon = lax.axis_index("lat"), lax.axis_index("lon")
    me = lat * lon_total + lon
    chips = devices // 2
    core, chip = me % 2, me // 2
    other = 1 - core

    def place(peer):
        return (peer // lon_total, peer % lon_total)

    barrier = pltpu.get_barrier_semaphore()

    def greet(k, _):
        pl.semaphore_signal(
            barrier, inc=1, device_id=place((me + k) % devices), device_id_type=pl.DeviceIdType.MESH
        )
        return 0

    lax.fori_loop(1, devices, greet, 0)

    def fill(i, _):
        grid[i, 0:cols, :] = own_ref[i].astype(f32)
        return 0

    lax.fori_loop(0, rows, fill, 0)
    pl.semaphore_wait(barrier, devices - 1)

    ways = ((-1, 0), (1, 0), (0, -1), (0, 1), (-1, -1), (-1, 1), (1, -1), (1, 1))
    halos = []
    for w, (da, db) in enumerate(ways):
        copy = pltpu.make_async_remote_copy(
            src_ref=strips[w],
            dst_ref=landed[w],
            send_sem=halo_send.at[w],
            recv_sem=halo_recv.at[w],
            device_id=((lat + da + lat_total) % lat_total, (lon + db + lon_total) % lon_total),
            device_id_type=pl.DeviceIdType.MESH,
        )
        sends = (lat + da >= 0) & (lat + da < lat_total)
        takes = (lat - da >= 0) & (lat - da < lat_total)
        halos.append((copy, sends, takes))

    def when(da, cond, fn):
        if da == 0:
            fn()
        else:
            pl.when(cond)(fn)

    for (copy, sends, _), (da, _) in zip(halos, ways):
        when(da, sends, copy.start)

    turned[:, 0 : 2 * tile_lon] = jnp.zeros((channels, 2 * tile_lon), bf16)
    turned[:, rows * tile_lon : (rows + 2) * tile_lon] = jnp.zeros((channels, 2 * tile_lon), bf16)

    def turn(p, _):
        turned[:, pl.ds(pl.multiple_of((p + 2) * tile_lon, tile_lon), tile_lon)] = feat_ref[p].T
        return 0

    lax.fori_loop(0, tile_lat, turn, 0)
    mixer[...] = jnp.zeros_like(mixer)
    for a in range(3):
        for b in range(3):
            tap = weight_ref[a, b].T
            for r in range(2):
                at = ((r + 2 - a) * 3 + b) * channels
                mixer[at : at + channels, r * channels : (r + 1) * channels] = tap
    total[...] = jnp.zeros_like(total)

    for (copy, _, takes), (da, db), ref in zip(halos, ways, landed):

        def take(copy=copy, da=da, db=db, ref=ref):
            copy.wait_recv()
            high = {-1: rows - up, 0: 0, 1: 0}[da]
            count = {-1: up, 0: rows, 1: down}[da]
            left = {-1: cols - up, 0: 0, 1: 0}[db]
            width = {-1: up, 0: cols, 1: down}[db]

            def add(i, _):
                grid[high + i, left : left + width, :] += ref[i].astype(f32)
                return 0

            lax.fori_loop(0, count, add, 0)

        when(da, takes, take)

    @pl.when(lat == 0)
    def _():
        grid[0] = jnp.zeros(grid.shape[1:], f32)

    @pl.when(lat == lat_total - 1)
    def _():
        grid[rows - 1] = jnp.zeros(grid.shape[1:], f32)

    def shift(i, _):
        at = pl.ds(pl.multiple_of(i * tile_lon, tile_lon), tile_lon)
        for b in range(3):
            windows[at, b * channels : (b + 1) * channels] = grid[
                i, 2 - b : 2 - b + tile_lon, :
            ].astype(bf16)
        return 0

    lax.fori_loop(0, rows, shift, 0)
    step = next(n for n in (11, 6, 3, 2, 1) if rows % n == 0)
    depth = step * tile_lon

    def weigh(k, _):
        start = k * depth
        lhs = jnp.concatenate(
            [
                turned[:, pl.ds(pl.multiple_of(start + a * tile_lon, tile_lon), depth)]
                for a in range(3)
            ],
            axis=0,
        )
        rhs = windows[pl.ds(pl.multiple_of(start, tile_lon), depth), :]
        total[...] += jnp.dot(lhs, rhs, preferred_element_type=f32)
        return 0

    lax.fori_loop(0, rows // step, weigh, 0)
    for a in range(3):
        for b in range(3):
            at = (a * 3 + b) * channels
            flat[at : at + channels, :] = total[
                a * channels : (a + 1) * channels, b * channels : (b + 1) * channels
            ]
    share = pieces.shape[1]

    def cut(d, _):
        pieces[d] = flat[pl.ds(d * share, share), :].astype(bf16)
        return 0

    lax.fori_loop(0, devices, cut, 0)
    part = math.gcd(tile_lat // 2, 8)
    strides = tile_lat // 2 // part
    first, second = strides // 4, strides * 3 // 4

    def apply(k, _):
        lhs = jnp.concatenate(
            [
                jnp.concatenate(
                    [
                        windows[
                            pl.ds(
                                pl.multiple_of((2 * (k * part + j) + r) * tile_lon, tile_lon),
                                tile_lon,
                            ),
                            :,
                        ]
                        for r in range(4)
                    ],
                    axis=1,
                )
                for j in range(part)
            ],
            axis=0,
        )
        acc = jnp.dot(lhs, mixer[...], preferred_element_type=f32).astype(bf16)
        for j in range(part):
            for r in range(2):
                ig_ref[2 * (k * part + j) + r] = acc[
                    j * tile_lon : (j + 1) * tile_lon, r * channels : (r + 1) * channels
                ]
        return 0

    def paired(src, dst, n):
        return pltpu.make_async_remote_copy(
            src_ref=src,
            dst_ref=dst,
            send_sem=pair_send.at[n],
            recv_sem=pair_recv.at[n],
            device_id=place(chip * 2 + other),
            device_id_type=pl.DeviceIdType.MESH,
        )

    def scattered(peer, slot):
        return pltpu.make_async_remote_copy(
            src_ref=pieces.at[core * chips + peer],
            dst_ref=parts.at[slot],
            send_sem=part_send.at[peer],
            recv_sem=part_recv.at[slot],
            device_id=place(peer * 2 + core),
            device_id_type=pl.DeviceIdType.MESH,
        )

    def shared(peer, slot):
        return pltpu.make_async_remote_copy(
            src_ref=mine,
            dst_ref=gathered.at[core * chips + slot],
            send_sem=all_send.at[peer],
            recv_sem=all_recv.at[slot],
            device_id=place(peer * 2 + core),
            device_id_type=pl.DeviceIdType.MESH,
        )

    def each(fn):
        def body(k, _):
            fn((chip + k) % chips)
            return 0

        lax.fori_loop(1, chips, body, 0)

    swap = paired(pieces.at[pl.ds(other * chips, chips)], twin, 0)
    swap.start()
    lax.fori_loop(0, first, apply, 0)
    swap.wait_recv()

    def merge(p, _):
        at = core * chips + p
        pieces[at] = (flat[pl.ds(at * share, share), :] + twin[p].astype(f32)).astype(bf16)
        return 0

    lax.fori_loop(0, chips, merge, 0)
    each(lambda peer: scattered(peer, chip).start())
    lax.fori_loop(first, second, apply, 0)
    parts[chip] = pieces[core * chips + chip]
    each(lambda peer: scattered(peer, peer).wait_recv())

    def gather_sum(p, acc):
        return acc + parts[p].astype(f32)

    mine[...] = lax.fori_loop(
        0, chips, gather_sum, jnp.zeros((share, channels), f32)
    ).astype(bf16)
    each(lambda peer: shared(peer, chip).start())
    gathered[core * chips + chip] = mine[...]
    lax.fori_loop(second, strides, apply, 0)
    each(lambda peer: shared(peer, peer).wait_recv())
    held = gathered.at[pl.ds(core * chips, chips)]
    back = paired(held, held, 1)
    back.start()

    def spill(d, _):
        wg_ref[pl.ds(d * share, share), :] = gathered[d].astype(f32)
        return 0

    lax.fori_loop(core * chips, (core + 1) * chips, spill, 0)
    back.wait_recv()
    lax.fori_loop(other * chips, (other + 1) * chips, spill, 0)
    for (copy, sends, _), (da, _) in zip(halos, ways):
        when(da, sends, copy.wait_send)
    swap.wait_send()
    back.wait_send()
    each(lambda peer: scattered(peer, chip).wait_send())
    each(lambda peer: shared(peer, chip).wait_send())


def shards(grad_rows, owner, lat_offset, lon_offset, position, live_count, features, conv_weight):
    lat_total = lax.axis_size("lat")
    lon_total = lax.axis_size("lon")
    device_total = lat_total * lon_total
    row_total, channels = grad_rows.shape
    tile_lat, tile_lon = features.shape[:2]
    capacity = max(2, 2 * row_total // device_total)
    smem = pl.BlockSpec(memory_space=pltpu.SMEM)
    vmem = pl.BlockSpec(memory_space=pltpu.VMEM)

    message = (device_total, capacity + geom_rows, channels)
    incoming = pl.pallas_call(
        functools.partial(pack_kernel, capacity, lat_total, lon_total),
        out_shape=jax.ShapeDtypeStruct(message, bf16),
        in_specs=[smem] + [vmem] * 5,
        out_specs=vmem,
        scratch_shapes=[
            pltpu.VMEM(message, bf16),
            pltpu.VMEM((device_total, channels), f32),
            pltpu.SemaphoreType.DMA((device_total,)),
            pltpu.SemaphoreType.DMA((device_total,)),
        ],
        compiler_params=pltpu.CompilerParams(
            vmem_limit_bytes=24 * 2**20, collective_id=1, has_side_effects=True
        ),
        name="pack",
    )(
        live_count,
        grad_rows,
        owner.reshape(1, row_total),
        lat_offset.reshape(1, row_total),
        lon_offset.reshape(1, row_total),
        position.T,
    )
    info = incoming[:, capacity : capacity + 5, :capacity].transpose(1, 0, 2).astype(f32)
    info = info.reshape(-1)

    rows, cols = tile_lat + 2, tile_lon + 2
    tall = tile_lat + taps - 1
    wide = -(-(tile_lon + taps - 1) // 8) * 8
    up, down = before + 1, after + 1
    lanes = math.gcd(capacity, 4)
    strip_shapes = [
        (up, cols),
        (down, cols),
        (rows, up),
        (rows, down),
        (up, up),
        (up, down),
        (down, up),
        (down, down),
    ]
    own, *strips = pl.pallas_call(
        functools.partial(scatter_kernel, capacity, lanes),
        out_shape=[
            jax.ShapeDtypeStruct(shape + (channels,), bf16)
            for shape in [(rows, cols)] + strip_shapes
        ],
        in_specs=[smem, vmem],
        out_specs=[vmem] * 9,
        scratch_shapes=[
            pltpu.VMEM((lanes, tall, wide, channels), f32),
            pltpu.VMEM((capacity, channels), f32),
        ],
        compiler_params=pltpu.CompilerParams(vmem_limit_bytes=32 * 2**20),
        name="scatter",
    )(
        info,
        incoming,
    )
    flat_rows = 9 * channels
    share = flat_rows // device_total
    ring = pltpu.VMEM((device_total, share, channels), bf16)
    half_ring = pltpu.VMEM((device_total // 2, share, channels), bf16)
    input_grad, weight_grad = pl.pallas_call(
        functools.partial(conv_kernel, lat_total, lon_total),
        out_shape=[
            jax.ShapeDtypeStruct((tile_lat, tile_lon, channels), bf16),
            jax.ShapeDtypeStruct((flat_rows, channels), f32),
        ],
        in_specs=[vmem] * 11,
        out_specs=[vmem] * 2,
        scratch_shapes=[pltpu.VMEM(shape + (channels,), bf16) for shape in strip_shapes]
        + [
            pltpu.VMEM((rows, -(-cols // 8) * 8, channels), f32),
            pltpu.VMEM((rows * tile_lon, 3 * channels), bf16),
            pltpu.VMEM((channels, (rows + 2) * tile_lon), bf16),
            pltpu.VMEM((3 * channels, 3 * channels), f32),
            pltpu.VMEM((flat_rows, channels), f32),
            pltpu.VMEM((4 * 3 * channels, 2 * channels), bf16),
            ring,
            half_ring,
            half_ring,
            pltpu.VMEM((share, channels), bf16),
            ring,
            pltpu.SemaphoreType.DMA((8,)),
            pltpu.SemaphoreType.DMA((8,)),
            pltpu.SemaphoreType.DMA((2,)),
            pltpu.SemaphoreType.DMA((2,)),
            pltpu.SemaphoreType.DMA((device_total // 2,)),
            pltpu.SemaphoreType.DMA((device_total // 2,)),
            pltpu.SemaphoreType.DMA((device_total // 2,)),
            pltpu.SemaphoreType.DMA((device_total // 2,)),
        ],
        compiler_params=pltpu.CompilerParams(
            vmem_limit_bytes=36 * 2**20, collective_id=0, has_side_effects=True
        ),
        name="conv",
    )(own, *strips, features, conv_weight)
    return input_grad, weight_grad.reshape(3, 3, channels, channels)


def solution(mesh):
    placed = (
        P(("lat", "lon"), None),
        P(("lat", "lon"), None),
        P(("lat", "lon")),
        P(("lat", "lon")),
        P(("lat", "lon"), None),
        P(("lat", "lon")),
        P("lat", "lon", None),
        P(),
    )
    return jax.shard_map(
        shards, mesh=mesh, in_specs=placed, out_specs=(P("lat", "lon", None), P()), check_vma=False
    )
```

```python
import functools
import math

import jax
import jax.numpy as jnp
from jax import lax
from jax.experimental import pallas as pl
from jax.experimental.pallas import tpu as pltpu
from jax.sharding import PartitionSpec as P

rbf_scale = 1.5
taps = 8
before = 3
after = taps - 1 - before
geom_rows = 8
f32 = jnp.float32
bf16 = jnp.bfloat16


def pack_kernel(
    capacity,
    lat_total,
    lon_total,
    live_ref,
    rows_ref,
    owner_ref,
    lat_ref,
    lon_ref,
    pos_ref,
    out_ref,
    held,
    tally,
    send_sem,
    recv_sem,
):
    devices = out_ref.shape[0]
    row_total, channels = rows_ref.shape
    me = lax.axis_index("lat") * lon_total + lax.axis_index("lon")

    def place(peer):
        return (peer // lon_total, peer % lon_total)

    barrier = pltpu.get_barrier_semaphore()

    def greet(k, _):
        pl.semaphore_signal(
            barrier, inc=1, device_id=place((me + k) % devices), device_id_type=pl.DeviceIdType.MESH
        )
        return 0

    lax.fori_loop(1, devices, greet, 0)
    live = lax.broadcasted_iota(jnp.int32, (1, row_total), 1) < live_ref[0]
    owner = jnp.where(live, owner_ref[...], devices)
    match = lax.broadcasted_iota(jnp.int32, (devices, row_total), 0) == owner
    match = jnp.where(match, 1.0, 0.0)
    tally[...] = jnp.broadcast_to(jnp.sum(match, axis=1, keepdims=True), tally.shape)
    upper = lax.broadcasted_iota(jnp.int32, (row_total, row_total), 0) < lax.broadcasted_iota(
        jnp.int32, (row_total, row_total), 1
    )
    upper = jnp.where(upper, 1.0, 0.0).astype(bf16)
    earlier = jnp.dot(match.astype(bf16), upper, preferred_element_type=f32)
    rank = jnp.sum(earlier * match, axis=0, keepdims=True).astype(jnp.int32)
    slot = owner * capacity + rank
    geometry = jnp.concatenate(
        [
            pos_ref[...].astype(f32),
            lat_ref[...].astype(f32),
            lon_ref[...].astype(f32),
            jnp.zeros((geom_rows - 4, row_total), f32),
        ],
        axis=0,
    ).astype(bf16)
    group = math.gcd(devices, max(1, 256 // capacity))
    groups = devices // group
    line = lax.broadcasted_iota(jnp.int32, (group * capacity, row_total), 0)
    row_line = lax.broadcasted_iota(jnp.int32, (geom_rows, capacity), 0)

    def build(first):
        hit = jnp.where(line == slot - first * capacity, 1.0, 0.0).astype(bf16)
        placed = jnp.dot(hit, rows_ref[...], preferred_element_type=f32).astype(bf16)
        info = lax.dot_general(
            geometry, hit, (((1,), (1,)), ((), ())), preferred_element_type=f32
        )
        for i in range(group):
            held[first + i, 0:capacity, :] = placed[i * capacity : (i + 1) * capacity]
            held[first + i, capacity : capacity + geom_rows, 0:capacity] = jnp.where(
                row_line == 4,
                tally[pl.ds(first + i, 1), 0:capacity],
                info[:, i * capacity : (i + 1) * capacity],
            ).astype(bf16)

    def copy_to(peer, slot_at):
        return pltpu.make_async_remote_copy(
            src_ref=held.at[peer],
            dst_ref=out_ref.at[slot_at],
            send_sem=send_sem.at[peer],
            recv_sem=recv_sem.at[slot_at],
            device_id=place(peer),
            device_id_type=pl.DeviceIdType.MESH,
        )

    def send(first):
        for i in range(group):
            peer = first + i

            @pl.when(peer != me)
            def _():
                copy_to(peer, me).start()

    odd = groups // 2

    def first_of(k):
        ahead = jnp.where(k < odd, 2 * k + 1, 2 * (k - odd))
        return ((me // group + ahead) % groups) * group

    build(first_of(0))
    pl.semaphore_wait(barrier, devices - 1)

    def work(k, _):
        build(first_of(k))
        send(first_of(k - 1))
        return 0

    lax.fori_loop(1, groups, work, 0)
    send(first_of(groups - 1))
    out_ref[me] = held[me]

    def each(fn):
        def body(k, _):
            fn((me + k) % devices)
            return 0

        lax.fori_loop(1, devices, body, 0)

    each(lambda peer: copy_to(peer, peer).wait_recv())
    each(lambda peer: copy_to(peer, me).wait_send())


def scatter_kernel(
    capacity,
    lanes,
    info_ref,
    msg_ref,
    own_ref,
    up_ref,
    down_ref,
    left_ref,
    right_ref,
    ul_ref,
    ur_ref,
    dl_ref,
    dr_ref,
    canvas,
    block,
):
    sources = msg_ref.shape[0]
    slots = sources * capacity
    rows, cols = own_ref.shape[0], own_ref.shape[1]
    tall = canvas.shape[1]
    inv = 1.0 / (2.0 * rbf_scale * rbf_scale)

    def clear(i, _):
        for j in range(lanes):
            canvas[j, i] = jnp.zeros(canvas.shape[2:], f32)
        return 0

    lax.fori_loop(0, tall, clear, 0)
    line = lax.broadcasted_iota(jnp.int32, (taps, canvas.shape[3]), 0).astype(f32) - before
    level = [math.exp(-((a - before) ** 2 - before**2) * inv) for a in range(taps)]

    def source(src, _):
        block[...] = msg_ref[src, 0:capacity, :].astype(f32)

        def prepare(i):
            terms = []
            for j in range(lanes):
                s = i * lanes + j
                at = src * capacity + s
                fa, fb = info_ref[at], info_ref[at + slots]
                d = line - fb
                t = jnp.exp(-(d * d + (before + fa) * (before + fa)) * inv) * block[pl.ds(s, 1), :]
                g = jnp.exp(jnp.full(t.shape, 2.0 * inv, f32) * fa)
                r = info_ref[at + 2 * slots].astype(jnp.int32)
                c = info_ref[at + 3 * slots].astype(jnp.int32)
                terms.append((r, c, t, g))
            return tuple(terms)

        trips = (info_ref[4 * slots + src * capacity].astype(jnp.int32) + lanes - 1) // lanes

        def step(i, terms):
            ahead = prepare(jnp.minimum(i + 1, trips - 1))
            sums = []
            for j, (r, c, t, g) in enumerate(terms):
                for a in range(taps):
                    sums.append(canvas[j, r + a, pl.ds(c, taps), :] + t * level[a])
                    t = t * g
            for j, (r, c, _, _) in enumerate(terms):
                for a in range(taps):
                    canvas[j, r + a, pl.ds(c, taps), :] = sums[j * taps + a]
            return ahead

        lax.fori_loop(0, trips, step, prepare(0))
        return 0

    lax.fori_loop(0, sources, source, 0)
    up, down = before + 1, after + 1
    inset = before - 1

    def total(i):
        whole = canvas[0, i]
        for j in range(1, lanes):
            whole = whole + canvas[j, i]
        canvas[0, i] = whole

    def finish(i, _):
        total(i)
        return 0

    lax.fori_loop(0, tall, finish, 0)

    def emit(i, _):
        own_ref[i] = canvas[0, i + inset, inset : inset + cols, :].astype(bf16)
        left_ref[i] = canvas[0, i + inset, 0:up, :].astype(bf16)
        right_ref[i] = canvas[0, i + inset, inset + cols - 2 : inset + cols - 2 + down, :].astype(bf16)
        return 0

    lax.fori_loop(0, rows, emit, 0)
    spans = ((0, up), (inset, cols), (inset + cols - 2, down))
    for count, first, refs in (
        (up, 0, (ul_ref, up_ref, ur_ref)),
        (down, inset + rows - 2, (dl_ref, down_ref, dr_ref)),
    ):
        for i in range(count):
            for (start, width), ref in zip(spans, refs):
                ref[i] = canvas[0, first + i, start : start + width, :].astype(bf16)


def conv_kernel(
    lat_total,
    lon_total,
    own_ref,
    *refs,
):
    strips, (feat_ref, weight_ref, ig_ref, wg_ref) = refs[:8], refs[8:12]
    landed = refs[12:20]
    (grid, windows, turned, total, flat, mixer, pieces, twin, parts, mine, gathered) = refs[20:31]
    halo_send, halo_recv, pair_send, pair_recv, part_send, part_recv, all_send, all_recv = refs[31:]
    rows, cols = own_ref.shape[0], own_ref.shape[1]
    tile_lat, tile_lon, channels = feat_ref.shape
    up, down = before + 1, after + 1
    devices = lat_total * lon_total
    lat, lon = lax.axis_index("lat"), lax.axis_index("lon")
    me = lat * lon_total + lon
    chips = devices // 2
    core, chip = me % 2, me // 2
    other = 1 - core

    def place(peer):
        return (peer // lon_total, peer % lon_total)

    barrier = pltpu.get_barrier_semaphore()

    def greet(k, _):
        pl.semaphore_signal(
            barrier, inc=1, device_id=place((me + k) % devices), device_id_type=pl.DeviceIdType.MESH
        )
        return 0

    lax.fori_loop(1, devices, greet, 0)

    def fill(i, _):
        grid[i, 0:cols, :] = own_ref[i].astype(f32)
        return 0

    lax.fori_loop(0, rows, fill, 0)
    pl.semaphore_wait(barrier, devices - 1)

    ways = ((-1, 0), (1, 0), (0, -1), (0, 1), (-1, -1), (-1, 1), (1, -1), (1, 1))
    halos = []
    for w, (da, db) in enumerate(ways):
        copy = pltpu.make_async_remote_copy(
            src_ref=strips[w],
            dst_ref=landed[w],
            send_sem=halo_send.at[w],
            recv_sem=halo_recv.at[w],
            device_id=((lat + da + lat_total) % lat_total, (lon + db + lon_total) % lon_total),
            device_id_type=pl.DeviceIdType.MESH,
        )
        sends = (lat + da >= 0) & (lat + da < lat_total)
        takes = (lat - da >= 0) & (lat - da < lat_total)
        halos.append((copy, sends, takes))

    def when(da, cond, fn):
        if da == 0:
            fn()
        else:
            pl.when(cond)(fn)

    for (copy, sends, _), (da, _) in zip(halos, ways):
        when(da, sends, copy.start)

    turned[:, 0 : 2 * tile_lon] = jnp.zeros((channels, 2 * tile_lon), bf16)
    turned[:, rows * tile_lon : (rows + 2) * tile_lon] = jnp.zeros((channels, 2 * tile_lon), bf16)

    def turn(p, _):
        turned[:, pl.ds(pl.multiple_of((p + 2) * tile_lon, tile_lon), tile_lon)] = feat_ref[p].T
        return 0

    lax.fori_loop(0, tile_lat, turn, 0)
    mixer[...] = jnp.zeros_like(mixer)
    for a in range(3):
        for b in range(3):
            tap = weight_ref[a, b].T
            for r in range(2):
                at = ((r + 2 - a) * 3 + b) * channels
                mixer[at : at + channels, r * channels : (r + 1) * channels] = tap
    total[...] = jnp.zeros_like(total)

    for (copy, _, takes), (da, db), ref in zip(halos, ways, landed):

        def take(copy=copy, da=da, db=db, ref=ref):
            copy.wait_recv()
            high = {-1: rows - up, 0: 0, 1: 0}[da]
            count = {-1: up, 0: rows, 1: down}[da]
            left = {-1: cols - up, 0: 0, 1: 0}[db]
            width = {-1: up, 0: cols, 1: down}[db]

            def add(i, _):
                grid[high + i, left : left + width, :] += ref[i].astype(f32)
                return 0

            lax.fori_loop(0, count, add, 0)

        when(da, takes, take)

    @pl.when(lat == 0)
    def _():
        grid[0] = jnp.zeros(grid.shape[1:], f32)

    @pl.when(lat == lat_total - 1)
    def _():
        grid[rows - 1] = jnp.zeros(grid.shape[1:], f32)

    def shift(i, _):
        at = pl.ds(pl.multiple_of(i * tile_lon, tile_lon), tile_lon)
        for b in range(3):
            windows[at, b * channels : (b + 1) * channels] = grid[
                i, 2 - b : 2 - b + tile_lon, :
            ].astype(bf16)
        return 0

    lax.fori_loop(0, rows, shift, 0)
    step = next(n for n in (11, 6, 3, 2, 1) if rows % n == 0)
    depth = step * tile_lon

    def weigh(k, _):
        start = k * depth
        lhs = jnp.concatenate(
            [
                turned[:, pl.ds(pl.multiple_of(start + a * tile_lon, tile_lon), depth)]
                for a in range(3)
            ],
            axis=0,
        )
        rhs = windows[pl.ds(pl.multiple_of(start, tile_lon), depth), :]
        total[...] += jnp.dot(lhs, rhs, preferred_element_type=f32)
        return 0

    lax.fori_loop(0, rows // step, weigh, 0)
    for a in range(3):
        for b in range(3):
            at = (a * 3 + b) * channels
            flat[at : at + channels, :] = total[
                a * channels : (a + 1) * channels, b * channels : (b + 1) * channels
            ]
    share = pieces.shape[1]

    def cut(d, _):
        pieces[d] = flat[pl.ds(d * share, share), :].astype(bf16)
        return 0

    lax.fori_loop(0, devices, cut, 0)
    part = math.gcd(tile_lat // 2, 8)
    strides = tile_lat // 2 // part
    first, second = strides // 4, strides * 3 // 4

    def apply(k, _):
        lhs = jnp.concatenate(
            [
                jnp.concatenate(
                    [
                        windows[
                            pl.ds(
                                pl.multiple_of((2 * (k * part + j) + r) * tile_lon, tile_lon),
                                tile_lon,
                            ),
                            :,
                        ]
                        for r in range(4)
                    ],
                    axis=1,
                )
                for j in range(part)
            ],
            axis=0,
        )
        acc = jnp.dot(lhs, mixer[...], preferred_element_type=f32).astype(bf16)
        for j in range(part):
            for r in range(2):
                ig_ref[2 * (k * part + j) + r] = acc[
                    j * tile_lon : (j + 1) * tile_lon, r * channels : (r + 1) * channels
                ]
        return 0

    def paired(src, dst, n):
        return pltpu.make_async_remote_copy(
            src_ref=src,
            dst_ref=dst,
            send_sem=pair_send.at[n],
            recv_sem=pair_recv.at[n],
            device_id=place(chip * 2 + other),
            device_id_type=pl.DeviceIdType.MESH,
        )

    def scattered(peer, slot):
        return pltpu.make_async_remote_copy(
            src_ref=pieces.at[core * chips + peer],
            dst_ref=parts.at[slot],
            send_sem=part_send.at[peer],
            recv_sem=part_recv.at[slot],
            device_id=place(peer * 2 + core),
            device_id_type=pl.DeviceIdType.MESH,
        )

    def shared(peer, slot):
        return pltpu.make_async_remote_copy(
            src_ref=mine,
            dst_ref=gathered.at[core * chips + slot],
            send_sem=all_send.at[peer],
            recv_sem=all_recv.at[slot],
            device_id=place(peer * 2 + core),
            device_id_type=pl.DeviceIdType.MESH,
        )

    def each(fn):
        def body(k, _):
            fn((chip + k) % chips)
            return 0

        lax.fori_loop(1, chips, body, 0)

    swap = paired(pieces.at[pl.ds(other * chips, chips)], twin, 0)
    swap.start()
    lax.fori_loop(0, first, apply, 0)
    swap.wait_recv()

    def merge(p, _):
        at = core * chips + p
        pieces[at] = (flat[pl.ds(at * share, share), :] + twin[p].astype(f32)).astype(bf16)
        return 0

    lax.fori_loop(0, chips, merge, 0)
    each(lambda peer: scattered(peer, chip).start())
    lax.fori_loop(first, second, apply, 0)
    parts[chip] = pieces[core * chips + chip]
    each(lambda peer: scattered(peer, peer).wait_recv())

    def gather_sum(p, acc):
        return acc + parts[p].astype(f32)

    mine[...] = lax.fori_loop(
        0, chips, gather_sum, jnp.zeros((share, channels), f32)
    ).astype(bf16)
    each(lambda peer: shared(peer, chip).start())
    gathered[core * chips + chip] = mine[...]
    lax.fori_loop(second, strides, apply, 0)
    each(lambda peer: shared(peer, peer).wait_recv())
    held = gathered.at[pl.ds(core * chips, chips)]
    back = paired(held, held, 1)
    back.start()

    def spill(d, _):
        wg_ref[pl.ds(d * share, share), :] = gathered[d].astype(f32)
        return 0

    lax.fori_loop(core * chips, (core + 1) * chips, spill, 0)
    back.wait_recv()
    lax.fori_loop(other * chips, (other + 1) * chips, spill, 0)
    for (copy, sends, _), (da, _) in zip(halos, ways):
        when(da, sends, copy.wait_send)
    swap.wait_send()
    back.wait_send()
    each(lambda peer: scattered(peer, chip).wait_send())
    each(lambda peer: shared(peer, chip).wait_send())


def shards(grad_rows, owner, lat_offset, lon_offset, position, live_count, features, conv_weight):
    lat_total = lax.axis_size("lat")
    lon_total = lax.axis_size("lon")
    device_total = lat_total * lon_total
    row_total, channels = grad_rows.shape
    tile_lat, tile_lon = features.shape[:2]
    capacity = max(2, 2 * row_total // device_total)
    smem = pl.BlockSpec(memory_space=pltpu.SMEM)
    vmem = pl.BlockSpec(memory_space=pltpu.VMEM)

    message = (device_total, capacity + geom_rows, channels)
    incoming = pl.pallas_call(
        functools.partial(pack_kernel, capacity, lat_total, lon_total),
        out_shape=jax.ShapeDtypeStruct(message, bf16),
        in_specs=[smem] + [vmem] * 5,
        out_specs=vmem,
        scratch_shapes=[
            pltpu.VMEM(message, bf16),
            pltpu.VMEM((device_total, channels), f32),
            pltpu.SemaphoreType.DMA((device_total,)),
            pltpu.SemaphoreType.DMA((device_total,)),
        ],
        compiler_params=pltpu.CompilerParams(
            vmem_limit_bytes=60 * 2**20, collective_id=1, has_side_effects=True
        ),
        name="pack",
    )(
        live_count,
        grad_rows,
        owner.reshape(1, row_total),
        lat_offset.reshape(1, row_total),
        lon_offset.reshape(1, row_total),
        position.T,
    )
    info = incoming[:, capacity : capacity + 5, :capacity].transpose(1, 0, 2).astype(f32)
    info = info.reshape(-1)

    rows, cols = tile_lat + 2, tile_lon + 2
    tall = tile_lat + taps - 1
    wide = -(-(tile_lon + taps - 1) // 8) * 8
    up, down = before + 1, after + 1
    lanes = math.gcd(capacity, 4)
    strip_shapes = [
        (up, cols),
        (down, cols),
        (rows, up),
        (rows, down),
        (up, up),
        (up, down),
        (down, up),
        (down, down),
    ]
    own, *strips = pl.pallas_call(
        functools.partial(scatter_kernel, capacity, lanes),
        out_shape=[
            jax.ShapeDtypeStruct(shape + (channels,), bf16)
            for shape in [(rows, cols)] + strip_shapes
        ],
        in_specs=[smem, vmem],
        out_specs=[vmem] * 9,
        scratch_shapes=[
            pltpu.VMEM((lanes, tall, wide, channels), f32),
            pltpu.VMEM((capacity, channels), f32),
        ],
        compiler_params=pltpu.CompilerParams(vmem_limit_bytes=32 * 2**20),
        name="scatter",
    )(
        info,
        incoming,
    )
    flat_rows = 9 * channels
    share = flat_rows // device_total
    ring = pltpu.VMEM((device_total, share, channels), bf16)
    half_ring = pltpu.VMEM((device_total // 2, share, channels), bf16)
    input_grad, weight_grad = pl.pallas_call(
        functools.partial(conv_kernel, lat_total, lon_total),
        out_shape=[
            jax.ShapeDtypeStruct((tile_lat, tile_lon, channels), bf16),
            jax.ShapeDtypeStruct((flat_rows, channels), f32),
        ],
        in_specs=[vmem] * 11,
        out_specs=[vmem] * 2,
        scratch_shapes=[pltpu.VMEM(shape + (channels,), bf16) for shape in strip_shapes]
        + [
            pltpu.VMEM((rows, -(-cols // 8) * 8, channels), f32),
            pltpu.VMEM((rows * tile_lon, 3 * channels), bf16),
            pltpu.VMEM((channels, (rows + 2) * tile_lon), bf16),
            pltpu.VMEM((3 * channels, 3 * channels), f32),
            pltpu.VMEM((flat_rows, channels), f32),
            pltpu.VMEM((4 * 3 * channels, 2 * channels), bf16),
            ring,
            half_ring,
            half_ring,
            pltpu.VMEM((share, channels), bf16),
            ring,
            pltpu.SemaphoreType.DMA((8,)),
            pltpu.SemaphoreType.DMA((8,)),
            pltpu.SemaphoreType.DMA((2,)),
            pltpu.SemaphoreType.DMA((2,)),
            pltpu.SemaphoreType.DMA((device_total // 2,)),
            pltpu.SemaphoreType.DMA((device_total // 2,)),
            pltpu.SemaphoreType.DMA((device_total // 2,)),
            pltpu.SemaphoreType.DMA((device_total // 2,)),
        ],
        compiler_params=pltpu.CompilerParams(
            vmem_limit_bytes=36 * 2**20, collective_id=0, has_side_effects=True
        ),
        name="conv",
    )(own, *strips, features, conv_weight)
    return input_grad, weight_grad.reshape(3, 3, channels, channels)


def solution(mesh):
    placed = (
        P(("lat", "lon"), None),
        P(("lat", "lon"), None),
        P(("lat", "lon")),
        P(("lat", "lon")),
        P(("lat", "lon"), None),
        P(("lat", "lon")),
        P("lat", "lon", None),
        P(),
    )
    return jax.shard_map(
        shards, mesh=mesh, in_specs=placed, out_specs=(P("lat", "lon", None), P()), check_vma=False
    )
```
